32 devices in a mesh: grp: 2 (over y), chan: 16 (over z, x, core).
Axes of the slice: x: 2, y: 2, z: 4, core: 2. Of those that a mesh axis runs over, the one named last changes fastest.
Arguments:
- volume: bfloat16 [32, 4, 32, 128, 64], P(('grp', 'chan')), parts along dimension 0, may hold values from -6 to 6
- first_filters: bfloat16 [3, 3, 3, 64, 256], replicated, may hold values from -0.15625 to 0.15625
- second_filters: bfloat16 [3, 3, 3, 256, 512], P(None, None, None, None, 'chan'), may hold values from -0.078125 to 0.078125
Outputs:
- features: bfloat16 [32, 1, 8, 32, 512], P(('grp', 'chan')), parts along dimension 0
The draws below stay inside these ranges and needn't reach their ends.
There are 2 independent parts, one for each index of `grp`. The reference program is written for one: setup_inputs(seed, part) draws one part's arguments, and reference() takes and returns one part's arrays. A program takes and returns all parts, laid end to end along the dimension named above; an argument that names none is the same for every part. Nothing has to cross between parts.
All inputs are finite; a program needn't handle non-finite values.
Results may differ from the reference program's by a relative error of at most 0.005.
Values may be sent and summed in bfloat16 or wider, within the bound.
A program may use at most 128 MiB of HBM per device.

```python
import jax
import jax.numpy as jnp
from jax import lax

SLAB = 4
YS = 32
ZC = 128
C0 = 64
C1 = 256
C2 = 512
BLOCKS = 16


def shard_levels(key, shape, shards, low, high):
    loudness, own = 1.0, jax.random.fold_in(key, 6)
    for axis_at, parts in shards:
        draws = jnp.exp(jax.random.uniform(jax.random.fold_in(own, axis_at), (parts,), jnp.float32, low / len(shards), high / len(shards)))
        loudness = loudness * jnp.repeat(draws, shape[axis_at] // parts).reshape([-1 if axis == axis_at else 1 for axis in range(len(shape))])
    return loudness


def gaussian(own_key, shape, deviation, most, cuts=(), held_as=jnp.bfloat16):
    entries = deviation * jax.random.normal(own_key, shape, jnp.float32)
    if cuts:
        entries = entries * shard_levels(own_key, shape, cuts, -0.22, 0.18)
    return jnp.clip(entries, -most, most).astype(held_as)


def setup_inputs(seed: int = 0, part: int = 0) -> dict:
    arg_keys = jax.random.split(jax.random.key(seed), 4)
    part_keys = jax.random.split(jax.random.fold_in(arg_keys[3], part), 4)
    volume = gaussian(part_keys[0], (BLOCKS, SLAB, YS, ZC, C0), 1.0, 6.0, ((0, 16),))
    first_filters = gaussian(arg_keys[1], (3, 3, 3, C0, C1), (27 * C0) ** -0.5, 0.15625)
    second_filters = gaussian(arg_keys[2], (3, 3, 3, C1, C2), (27 * C1) ** -0.5, 0.078125, ((4, 16),))
    return {"volume": volume, "first_filters": first_filters, "second_filters": second_filters}


def leaky_relu(values):
    return jnp.where(values > 0, values, 0.3 * values)


def strided_conv(inputs, filters):
    result = lax.conv_general_dilated(
        inputs.astype(jnp.float32)[None], filters.astype(jnp.float32),
        window_strides=(2, 2, 2), padding=((0, 1), (0, 1), (0, 1)),
        dimension_numbers=("NDHWC", "DHWIO", "NDHWC"),
        precision=lax.Precision.HIGHEST)
    return result[0]


def reference(volume, first_filters, second_filters):
    block_count, slab_cells, row_cells, depth_cells, in_channels = volume.shape
    whole = volume.reshape(block_count * slab_cells, row_cells, depth_cells, in_channels)
    hidden = leaky_relu(strided_conv(whole, first_filters)).astype(jnp.bfloat16)
    result = leaky_relu(strided_conv(hidden, second_filters)).astype(jnp.bfloat16)
    out_channels = second_filters.shape[4]
    return result.reshape(block_count, slab_cells // 4, row_cells // 4, depth_cells // 4, out_channels)
```

```python
import jax
import jax.numpy as jnp
from jax import lax
from jax.experimental import pallas as pl
from jax.experimental.pallas import tpu as pltpu
from jax.sharding import PartitionSpec as P

F32 = jnp.float32
BF16 = jnp.bfloat16
VMEM_BYTES = 56 * 1024 * 1024


def passed_along(value, axis, steps):
    count = lax.axis_size(axis)
    initial, last = (max(0, -steps), min(count, count - steps))
    return lax.ppermute(value, axis, [(source, source + steps) for source in range(initial, last)])


def leaky_relu(values):
    return jnp.where(values > 0, values, 0.3 * values)


def shifted_up(values, period):
    count = values.shape[0]
    moved = pltpu.roll(values, count - 1, 0)
    row = lax.broadcasted_iota(jnp.int32, values.shape, 0)
    return jnp.where(row % period == period - 1, 0.0, moved)


def taps_of_plane(source, source_plane, taps, plane):
    pairs, depth = source.shape[1] // 2, source.shape[2]

    def body(pair, carry):
        for parity in range(2):
            cells = source[source_plane, 2 * pair + parity]
            moved = shifted_up(cells.astype(F32), depth).astype(BF16)
            taps[plane, parity, pair] = jnp.concatenate([cells, moved], axis=-1)
        return carry

    lax.fori_loop(0, pairs, body, 0)


def zero_row(taps, plane):
    taps[plane, 0, taps.shape[2] - 1] = jnp.zeros(taps.shape[3:], BF16)


def conv_first(taps, filters, held, hidden, plane, part, parts):
    rows = hidden.shape[3] * 2 // parts
    depth, width = taps.shape[3:]
    total = None
    for i in range(3):
        for j in range(3):
            lhs = taps[2 * plane + i, j % 2, pl.ds(part * rows + j // 2, rows)]
            term = jnp.dot(lhs.reshape(rows * depth, width), filters[3 * i + j], preferred_element_type=F32)
            total = term if total is None else total + term
    total = leaky_relu(total).astype(BF16).astype(F32)
    half = rows * depth // 2
    channels = hidden.shape[5]
    blocks = channels // 128
    for block in range(blocks):
        held[block] = total[:, block * 128 : block * 128 + 128]
    for k in range(2):
        cells = jnp.concatenate([held[block, pl.ds(k, half, stride=2)] for block in range(blocks)], axis=-1)
        pieces = [cells] if k else [cells, shifted_up(cells, depth // 2)]
        for at, piece in zip((k, 2), pieces):
            piece = piece.astype(BF16).reshape(rows // 2, 2, depth // 2, channels)
            for parity in range(2):
                hidden[plane, at, parity, pl.ds(part * rows // 2, rows // 2)] = piece[:, parity]


def conv_second(tap, filters, out):
    width = 256 if out.shape[1] % 256 == 0 else out.shape[1]
    for at in range(out.shape[1] // width):
        total = None
        for i in range(3):
            for j in range(3):
                for k in range(3):
                    rhs = filters[9 * i + 3 * j + k, pl.ds(at * width, width)]
                    term = lax.dot_general(
                        tap(i, j, k), rhs, (((1,), (1,)), ((), ())), preferred_element_type=F32
                    )
                    total = term if total is None else total + term
        out[:, pl.ds(at * width, width)] = leaky_relu(total).astype(BF16)


def first_kernel(cells, rim, filters, hidden, taps, held):
    planes = cells.shape[0]
    for plane in range(planes + 1):
        taps_of_plane(cells if plane < planes else rim, plane % planes, taps, plane)
        zero_row(taps, plane)
    for plane in range(planes // 2):
        for part in range(2):
            conv_first(taps, filters, held, hidden, plane, part, 2)


def padded_rows(hidden, rim, padded):
    planes = hidden.shape[0]
    rows = hidden.shape[3]
    for plane in range(planes + 1):
        for k in range(3):
            padded[plane, k, :, pl.ds(0, rows)] = hidden[plane, k] if plane < planes else rim[0, k]
            padded[plane, k, 0, rows] = jnp.zeros(padded.shape[4:], BF16)


def tap_reader(padded, rows):
    depth, channels = padded.shape[4:]

    def tap(i, j, k):
        return padded[i, k, j % 2, pl.ds(j // 2, rows)].reshape(rows * depth, channels)

    return tap


def second_kernel(hidden, rim, filters, out, padded):
    padded_rows(hidden, rim, padded)
    conv_second(tap_reader(padded, hidden.shape[3]), filters, out)


def whole_vmem(count):
    return [pl.BlockSpec(memory_space=pltpu.VMEM)] * count


def padded_first(first_filters):
    kernel, in_channels, out_channels = first_filters.shape[2:]
    flat = first_filters.reshape(9, kernel * in_channels, out_channels)
    return jnp.pad(flat, ((0, 0), (0, in_channels), (0, 0)))


def plain_shards(volume, first_filters, second_filters):
    planes, rows, depth, in_channels = volume.shape[1:]
    mid = first_filters.shape[4]
    turned = jnp.transpose(second_filters, (0, 1, 2, 4, 3)).reshape(27, second_filters.shape[4], mid)
    gathered = lax.all_gather(turned, "chan", axis=1, tiled=True)
    cells = volume.reshape(planes, rows, depth // 2, 2 * in_channels)
    rim = passed_along(cells[:1], "chan", -1)
    filters = padded_first(first_filters)
    hidden_shape = (planes // 2, 3, 2, rows // 4, depth // 4, mid)
    hidden = pl.pallas_call(
        first_kernel,
        out_shape=jax.ShapeDtypeStruct(hidden_shape, BF16),
        in_specs=whole_vmem(3),
        out_specs=whole_vmem(1)[0],
        scratch_shapes=[
            pltpu.VMEM((planes + 1, 2, rows // 2 + 1, depth // 2, 4 * in_channels), BF16),
            pltpu.VMEM((mid // 128, rows // 4 * (depth // 2), 128), F32),
        ],
        compiler_params=pltpu.CompilerParams(vmem_limit_bytes=VMEM_BYTES),
    )(cells, rim, filters)
    hidden_rim = passed_along(hidden[:1], "chan", -1)
    out_cells = rows // 4 * (depth // 4)
    out_channels = gathered.shape[1]
    result = pl.pallas_call(
        second_kernel,
        out_shape=jax.ShapeDtypeStruct((out_cells, out_channels), BF16),
        in_specs=whole_vmem(3),
        out_specs=whole_vmem(1)[0],
        scratch_shapes=[
            pltpu.VMEM((planes // 2 + 1, 3, 2, rows // 4 + 1, depth // 4, mid), BF16),
        ],
        compiler_params=pltpu.CompilerParams(vmem_limit_bytes=VMEM_BYTES),
    )(hidden, hidden_rim, gathered)
    return result.reshape(1, planes // 4, rows // 4, depth // 4, out_channels)


def position_of(chip, chips):
    column, along = chip % 2, chip // 2
    return along * (1 - column) + (chips - 1 - along) * column


def chip_at(position, chips):
    upper = position // (chips // 2)
    return (1 - upper) * 2 * position + upper * (2 * (chips - 1 - position) + 1)


def fold_pairs(cells, turned, taps, plane):
    pairs = cells.shape[1] // 2
    channels, depth = cells.shape[2:]
    slots = turned.shape[0]

    def body(step, carry):
        for slot in range(slots):
            pair = step * slots + slot
            both = cells[plane, pl.ds(2 * pair, 2)].reshape(2 * channels, depth)
            turned[slot] = both.astype(F32).T
            even = turned[slot, pl.ds(0, depth // 2, stride=2)]
            odd = turned[slot, pl.ds(1, depth // 2, stride=2)]
            later = shifted_up(even, depth // 2)
            taps[plane, pair] = jnp.concatenate([even, odd, later], axis=-1).astype(BF16)
        return carry

    lax.fori_loop(0, pairs // slots, body, 0)
    taps[plane, pairs] = jnp.zeros(taps.shape[2:], BF16)


def pack_first(filters, packed):
    channels, out_channels = filters.shape[1:]
    for i in range(3):
        for k in range(3):
            for j in range(2):
                packed[i, pl.ds((2 * k + j) * channels, channels)] = filters[9 * i + 3 * j + k]
            packed[i, pl.ds((6 + 2 * k) * channels, channels)] = filters[9 * i + 6 + k]
            packed[i, pl.ds((7 + 2 * k) * channels, channels)] = jnp.zeros((channels, out_channels), BF16)


def conv_pairs(taps, packed, held, padded, plane, part, parts):
    rows = (taps.shape[1] - 1) // parts
    depth, width = taps.shape[2:]
    channels = packed.shape[2]
    total = None
    for i in range(3):
        here = taps[2 * plane + i, pl.ds(part * rows, rows)].reshape(rows * depth, width)
        below = taps[2 * plane + i, pl.ds(part * rows + 1, rows)].reshape(rows * depth, width)
        lhs = jnp.concatenate([here, below], axis=-1)
        term = jnp.dot(lhs, packed[i], preferred_element_type=F32)
        total = term if total is None else total + term
    total = leaky_relu(total).astype(BF16).astype(F32)
    half = rows * depth // 2
    blocks = channels // 128
    for block in range(blocks):
        held[block] = total[:, block * 128 : block * 128 + 128]
    for k in range(2):
        cells = jnp.concatenate([held[block, pl.ds(k, half, stride=2)] for block in range(blocks)], axis=-1)
        pieces = [cells] if k else [cells, shifted_up(cells, depth // 2)]
        for at, piece in zip((k, 2), pieces):
            piece = piece.astype(BF16).reshape(rows // 2, 2, depth // 2, channels)
            for parity in range(2):
                padded[plane, at, parity, pl.ds(part * rows // 2, rows // 2)] = piece[:, parity]


STEPS = ((2, 1), (0, 1), (1, 1), (2, 2), (0, 2), (2, 3), (1, 2), (2, 4), (0, 3), (1, 3), (0, 4), (1, 4))
LAG = 2


def third_sum(i, lanes, blocks, tap, plane, filters):
    own_rows = filters.shape[2] // 9
    added = None
    for j in range(3):
        for k in range(3):
            rhs = filters[i, pl.ds(lanes, blocks), pl.ds((3 * j + k) * own_rows, own_rows)]
            term = lax.dot_general(
                tap(plane, j, k), rhs.reshape(blocks * own_rows, rhs.shape[2]), (((1,), (1,)), ((), ())),
                preferred_element_type=F32,
            )
            added = term if added is None else added + term
    return added


def ring_kernel(
    volume, first, shard, out,
    cells, first_held, packed, turned, taps, held, padded, filters, total, part_out, part_in,
    local_sem, ring_send, ring_recv, cross_send, cross_recv, side_send, side_recv,
    home_send, home_recv, rim_send, rim_recv,
):
    count = lax.axis_size("chan")
    chips = count // 2
    me = lax.axis_index("chan")
    grp = lax.axis_index("grp")
    core, chip = me % 2, me // 2
    spot = position_of(chip, chips)
    sibling = me + 1 - 2 * core
    right = 2 * chip_at((spot + 1) % chips, chips) + core
    left = 2 * chip_at((spot + chips - 1) % chips, chips) + core
    before, after = (me + count - 1) % count, (me + 1) % count
    planes = volume.shape[0]
    far = chips // 2
    piece = shard.shape[1]
    carried = piece * 10 // 18
    crossed = piece - carried
    halved = piece // 2
    is_first, is_last = me == 0, me == count - 1

    local = [pltpu.make_async_copy(shard, filters.at[:, me], local_sem.at[0])]
    local.append(pltpu.make_async_copy(first, first_held, local_sem.at[1]))
    for plane in range(planes):
        local.append(pltpu.make_async_copy(volume.at[plane], cells.at[plane], local_sem.at[2 + plane]))
    for copy in local[1:3]:
        copy.start()

    barrier = pltpu.get_barrier_semaphore()
    peers = [{"chan": peer} for peer in (left, right, sibling, before, after)] + [{"grp": 1 - grp}]
    for peer in peers:
        pl.semaphore_signal(barrier, inc=1, device_id=peer, device_id_type=pl.DeviceIdType.MESH)
    pl.semaphore_wait(barrier, len(peers))

    def remote(source, target, send, recv, peer):
        return pltpu.make_async_remote_copy(
            src_ref=source, dst_ref=target, send_sem=send, recv_sem=recv,
            device_id=peer, device_id_type=pl.DeviceIdType.MESH,
        )

    def rows_at(offset, size):
        return pl.ds(pl.multiple_of(offset, 16), size)

    def unit_of(way, gone):
        return 2 * chip_at((spot + (chips - gone if way == 0 else gone)) % chips, chips) + core

    def ring_rows(way, gone):
        upper = grp if way == 0 else 1 - grp
        if gone < far:
            return rows_at(upper * crossed, carried)
        return rows_at(upper * halved, halved)

    def ring(way, t, gone):
        unit, rows = unit_of(way, gone - 1), ring_rows(way, gone)
        target = filters.at[t, unit, rows]
        source = shard.at[t, rows] if gone == 1 else target
        return remote(
            source, target, ring_send.at[way, t, gone - 1], ring_recv.at[way, t, gone - 1],
            {"chan": (right, left)[way]},
        )

    def arrival(way, t, gone):
        target = filters.at[t, unit_of(way, gone), ring_rows(way, gone)]
        return remote(
            target, target, ring_send.at[way, t, gone - 1], ring_recv.at[way, t, gone - 1], {"chan": left}
        )

    def cross(way, t, gone):
        upper = grp if way == 0 else 1 - grp
        block = filters.at[t, unit_of(way, gone), rows_at(upper * carried, crossed)]
        at = 2 * (gone - 1) + way
        return remote(block, block, cross_send.at[t, at], cross_recv.at[t, at], {"grp": 1 - grp})

    def side(way, t, gone):
        block = filters.at[t, unit_of(way, gone)]
        return remote(block, block, side_send.at[t], side_recv.at[t], {"chan": sibling})

    home = remote(shard, filters.at[:, me], home_send.at[0], home_recv.at[0], {"chan": sibling})
    rim = remote(volume.at[0], cells.at[planes], rim_send.at[0], rim_recv.at[0], {"chan": before})
    part = remote(part_out, part_in, rim_send.at[1], rim_recv.at[1], {"chan": before})

    for t, gone in STEPS:
        if gone == 1:
            for way in range(2):
                ring(way, t, 1).start()

    @pl.when(jnp.logical_not(is_first))
    def _():
        rim.start()

    home.start()
    for copy in local[3:] + local[:1]:
        copy.start()

    def serve(t, gone):
        for way in range(2):
            arrival(way, t, gone).wait_recv()
            if gone < far:
                ring(way, t, gone + 1).start()
                cross(way, t, gone).start()
        if gone == far:
            side(0, t, gone).start()

    def pass_on(t, gone):
        for way in range(2 if gone < far else 0):
            cross(way, t, gone).wait_recv()
            side(way, t, gone).start()

    def all_sides(t):
        block = filters.at[t, pl.ds(0, chips - 1)]
        return remote(block, block, side_send.at[t], side_recv.at[t], {"chan": sibling})

    def all_here(t):
        all_sides(t).wait_recv()

    def all_sent(t):
        for way in range(2):
            for gone in range(1, far + 1):
                ring(way, t, gone).wait_send()
            for gone in range(1, far):
                cross(way, t, gone).wait_send()
        all_sides(t).wait_send()

    tap = tap_reader(padded, padded.shape[3] - 1)
    blocks = filters.shape[1] // 2
    half = blocks * shard.shape[1] // 9
    lanes = [(at * blocks, pl.ds(at * half, half)) for at in range(2)]

    def start_work():
        local[1].wait()
        pack_first(first_held, packed)
        local[2].wait()
        fold_pairs(cells, turned, taps, 0)
        blank = jnp.zeros(padded.shape[4:], BF16)
        for plane in range(planes // 2):
            for k in range(3):
                padded[plane, k, 0, padded.shape[3] - 1] = blank

    def fold_plane(plane):
        local[2 + plane].wait()
        fold_pairs(cells, turned, taps, plane)

    def hidden_part(plane, at):
        conv_pairs(taps, packed, held, padded, plane, at, 2)

    def fold_rim():
        @pl.when(jnp.logical_not(is_last))
        def _():
            rim.wait_recv()

        @pl.when(is_last)
        def _():
            cells[planes] = jnp.zeros(cells.shape[1:], BF16)
            part_in[...] = jnp.zeros(part_in.shape, BF16)

        fold_pairs(cells, turned, taps, planes)

    def sum_for_before():
        home.wait_recv()
        local[0].wait()
        all_here(2)
        for at, columns in lanes:
            part_out[:, columns] = third_sum(2, at, blocks, tap, 0, filters).astype(BF16)

        @pl.when(jnp.logical_not(is_first))
        def _():
            part.start()

    def sum_of_first():
        all_here(0)
        for at, columns in lanes:
            total[:, columns] = third_sum(0, at, blocks, tap, 0, filters)

    def sum_of_second():
        @pl.when(jnp.logical_not(is_last))
        def _():
            part.wait_recv()

        all_here(1)
        for at, columns in lanes:
            added = total[:, columns] + part_in[:, columns].astype(F32)
            out[:, columns] = leaky_relu(third_sum(1, at, blocks, tap, 1, filters) + added).astype(BF16)

    work = {
        0: [start_work, lambda: fold_plane(1)],
        1: [lambda: fold_plane(2)],
        2: [lambda: hidden_part(0, 0)],
        3: [lambda: hidden_part(0, 1)],
        5: [lambda: fold_plane(3)],
        6: [fold_rim],
        7: [lambda: hidden_part(1, 0)],
        8: [lambda: hidden_part(1, 1)],
        10: [sum_for_before],
        11 + LAG: [sum_of_first],
    }
    for step in range(len(STEPS) + LAG):
        for item in work.get(step, []):
            item()
        if step < len(STEPS):
            serve(*STEPS[step])
        if step >= LAG:
            pass_on(*STEPS[step - LAG])

    sum_of_second()
    for t in range(3):
        all_sent(t)
    home.wait_send()

    @pl.when(jnp.logical_not(is_first))
    def _():
        rim.wait_send()
        part.wait_send()


def ring_shards(volume, first_filters, second_filters):
    planes, rows, depth, in_channels = volume.shape[1:]
    mid = first_filters.shape[4]
    own = second_filters.shape[4]
    count = lax.axis_size("chan")
    turned_cells = jnp.transpose(volume[0], (0, 1, 3, 2))
    turned_shard = jnp.transpose(second_filters, (0, 1, 2, 4, 3)).reshape(3, 9 * own, mid)
    out_cells = rows // 4 * (depth // 4)
    dma = pltpu.SemaphoreType.DMA
    result = pl.pallas_call(
        ring_kernel,
        out_shape=jax.ShapeDtypeStruct((out_cells, own * count), BF16),
        in_specs=[pl.BlockSpec(memory_space=pl.ANY)] * 3,
        out_specs=whole_vmem(1)[0],
        scratch_shapes=[
            pltpu.VMEM((planes + 1, rows, in_channels, depth), BF16),
            pltpu.VMEM((27, in_channels, mid), BF16),
            pltpu.VMEM((3, 12 * in_channels, mid), BF16),
            pltpu.VMEM((4, depth, 2 * in_channels), F32),
            pltpu.VMEM((planes + 1, rows // 2 + 1, depth // 2, 6 * in_channels), BF16),
            pltpu.VMEM((mid // 128, rows // 4 * (depth // 2), 128), F32),
            pltpu.VMEM((planes // 2, 3, 2, rows // 4 + 1, depth // 4, mid), BF16),
            pltpu.VMEM((3, count, 9 * own, mid), BF16),
            pltpu.VMEM((out_cells, own * count), F32),
            pltpu.VMEM((out_cells, own * count), BF16),
            pltpu.VMEM((out_cells, own * count), BF16),
            dma((2 + planes,)),
            *[dma((2, 3, count // 4))] * 2,
            *[dma((3, count // 2 - 2))] * 2,
            *[dma((3,))] * 2,
            *[dma((1,))] * 2,
            *[dma((2,))] * 2,
        ],
        compiler_params=pltpu.CompilerParams(
            vmem_limit_bytes=VMEM_BYTES, collective_id=0, has_side_effects=True
        ),
    )(turned_cells, first_filters.reshape(27, in_channels, mid), turned_shard)
    return result.reshape(1, planes // 4, rows // 4, depth // 4, own * count)


def shards(volume, first_filters, second_filters):
    fits = lax.axis_size("chan") == 16 and lax.axis_size("grp") == 2
    if fits and second_filters.shape[4] % 32 == 0 and volume.shape[1] == 4:
        return ring_shards(volume, first_filters, second_filters)
    return plain_shards(volume, first_filters, second_filters)


def solution(mesh):
    placed = (P(("grp", "chan"), None, None, None, None), P(), P(None, None, None, None, "chan"))
    return jax.shard_map(
        shards,
        mesh=mesh,
        in_specs=placed,
        out_specs=P(("grp", "chan"), None, None, None, None),
        check_vma=False,
    )
```

```python
import jax
import jax.numpy as jnp
from jax import lax
from jax.experimental import pallas as pl
from jax.experimental.pallas import tpu as pltpu
from jax.sharding import PartitionSpec as P

F32 = jnp.float32
BF16 = jnp.bfloat16
VMEM_BYTES = 56 * 1024 * 1024


def passed_along(value, axis, steps):
    count = lax.axis_size(axis)
    initial, last = (max(0, -steps), min(count, count - steps))
    return lax.ppermute(value, axis, [(source, source + steps) for source in range(initial, last)])


def leaky_relu(values):
    return jnp.where(values > 0, values, 0.3 * values)


def shifted_up(values, period):
    count = values.shape[0]
    moved = pltpu.roll(values, count - 1, 0)
    row = lax.broadcasted_iota(jnp.int32, values.shape, 0)
    return jnp.where(row % period == period - 1, 0.0, moved)


def taps_of_plane(source, source_plane, taps, plane):
    pairs, depth = source.shape[1] // 2, source.shape[2]

    def body(pair, carry):
        for parity in range(2):
            cells = source[source_plane, 2 * pair + parity]
            moved = shifted_up(cells.astype(F32), depth).astype(BF16)
            taps[plane, parity, pair] = jnp.concatenate([cells, moved], axis=-1)
        return carry

    lax.fori_loop(0, pairs, body, 0)


def zero_row(taps, plane):
    taps[plane, 0, taps.shape[2] - 1] = jnp.zeros(taps.shape[3:], BF16)


def conv_first(taps, filters, held, hidden, plane, part, parts):
    rows = hidden.shape[3] * 2 // parts
    depth, width = taps.shape[3:]
    total = None
    for i in range(3):
        for j in range(3):
            lhs = taps[2 * plane + i, j % 2, pl.ds(part * rows + j // 2, rows)]
            term = jnp.dot(lhs.reshape(rows * depth, width), filters[3 * i + j], preferred_element_type=F32)
            total = term if total is None else total + term
    total = leaky_relu(total).astype(BF16).astype(F32)
    half = rows * depth // 2
    channels = hidden.shape[5]
    blocks = channels // 128
    for block in range(blocks):
        held[block] = total[:, block * 128 : block * 128 + 128]
    for k in range(2):
        cells = jnp.concatenate([held[block, pl.ds(k, half, stride=2)] for block in range(blocks)], axis=-1)
        pieces = [cells] if k else [cells, shifted_up(cells, depth // 2)]
        for at, piece in zip((k, 2), pieces):
            piece = piece.astype(BF16).reshape(rows // 2, 2, depth // 2, channels)
            for parity in range(2):
                hidden[plane, at, parity, pl.ds(part * rows // 2, rows // 2)] = piece[:, parity]


def conv_second(tap, filters, out):
    width = 256 if out.shape[1] % 256 == 0 else out.shape[1]
    for at in range(out.shape[1] // width):
        total = None
        for i in range(3):
            for j in range(3):
                for k in range(3):
                    rhs = filters[9 * i + 3 * j + k, pl.ds(at * width, width)]
                    term = lax.dot_general(
                        tap(i, j, k), rhs, (((1,), (1,)), ((), ())), preferred_element_type=F32
                    )
                    total = term if total is None else total + term
        out[:, pl.ds(at * width, width)] = leaky_relu(total).astype(BF16)


def first_kernel(cells, rim, filters, hidden, taps, held):
    planes = cells.shape[0]
    for plane in range(planes + 1):
        taps_of_plane(cells if plane < planes else rim, plane % planes, taps, plane)
        zero_row(taps, plane)
    for plane in range(planes // 2):
        for part in range(2):
            conv_first(taps, filters, held, hidden, plane, part, 2)


def padded_rows(hidden, rim, padded):
    planes = hidden.shape[0]
    rows = hidden.shape[3]
    for plane in range(planes + 1):
        for k in range(3):
            padded[plane, k, :, pl.ds(0, rows)] = hidden[plane, k] if plane < planes else rim[0, k]
            padded[plane, k, 0, rows] = jnp.zeros(padded.shape[4:], BF16)


def tap_reader(padded, rows):
    depth, channels = padded.shape[4:]

    def tap(i, j, k):
        return padded[i, k, j % 2, pl.ds(j // 2, rows)].reshape(rows * depth, channels)

    return tap


def second_kernel(hidden, rim, filters, out, padded):
    padded_rows(hidden, rim, padded)
    conv_second(tap_reader(padded, hidden.shape[3]), filters, out)


def whole_vmem(count):
    return [pl.BlockSpec(memory_space=pltpu.VMEM)] * count


def padded_first(first_filters):
    kernel, in_channels, out_channels = first_filters.shape[2:]
    flat = first_filters.reshape(9, kernel * in_channels, out_channels)
    return jnp.pad(flat, ((0, 0), (0, in_channels), (0, 0)))


def plain_shards(volume, first_filters, second_filters):
    planes, rows, depth, in_channels = volume.shape[1:]
    mid = first_filters.shape[4]
    turned = jnp.transpose(second_filters, (0, 1, 2, 4, 3)).reshape(27, second_filters.shape[4], mid)
    gathered = lax.all_gather(turned, "chan", axis=1, tiled=True)
    cells = volume.reshape(planes, rows, depth // 2, 2 * in_channels)
    rim = passed_along(cells[:1], "chan", -1)
    filters = padded_first(first_filters)
    hidden_shape = (planes // 2, 3, 2, rows // 4, depth // 4, mid)
    hidden = pl.pallas_call(
        first_kernel,
        out_shape=jax.ShapeDtypeStruct(hidden_shape, BF16),
        in_specs=whole_vmem(3),
        out_specs=whole_vmem(1)[0],
        scratch_shapes=[
            pltpu.VMEM((planes + 1, 2, rows // 2 + 1, depth // 2, 4 * in_channels), BF16),
            pltpu.VMEM((mid // 128, rows // 4 * (depth // 2), 128), F32),
        ],
        compiler_params=pltpu.CompilerParams(vmem_limit_bytes=VMEM_BYTES),
    )(cells, rim, filters)
    hidden_rim = passed_along(hidden[:1], "chan", -1)
    out_cells = rows // 4 * (depth // 4)
    out_channels = gathered.shape[1]
    result = pl.pallas_call(
        second_kernel,
        out_shape=jax.ShapeDtypeStruct((out_cells, out_channels), BF16),
        in_specs=whole_vmem(3),
        out_specs=whole_vmem(1)[0],
        scratch_shapes=[
            pltpu.VMEM((planes // 2 + 1, 3, 2, rows // 4 + 1, depth // 4, mid), BF16),
        ],
        compiler_params=pltpu.CompilerParams(vmem_limit_bytes=VMEM_BYTES),
    )(hidden, hidden_rim, gathered)
    return result.reshape(1, planes // 4, rows // 4, depth // 4, out_channels)


def position_of(chip, chips):
    column, along = chip % 2, chip // 2
    return along * (1 - column) + (chips - 1 - along) * column


def chip_at(position, chips):
    upper = position // (chips // 2)
    return (1 - upper) * 2 * position + upper * (2 * (chips - 1 - position) + 1)


def fold_pairs(cells, turned, taps, plane):
    pairs = cells.shape[1] // 2
    channels, depth = cells.shape[2:]
    slots = turned.shape[0]

    def body(step, carry):
        for slot in range(slots):
            pair = step * slots + slot
            both = cells[plane, pl.ds(2 * pair, 2)].reshape(2 * channels, depth)
            turned[slot] = both.astype(F32).T
            even = turned[slot, pl.ds(0, depth // 2, stride=2)]
            odd = turned[slot, pl.ds(1, depth // 2, stride=2)]
            later = shifted_up(even, depth // 2)
            taps[plane, pair] = jnp.concatenate([even, odd, later], axis=-1).astype(BF16)
        return carry

    lax.fori_loop(0, pairs // slots, body, 0)
    taps[plane, pairs] = jnp.zeros(taps.shape[2:], BF16)


def pack_first(filters, packed):
    channels, out_channels = filters.shape[1:]
    for i in range(3):
        for k in range(3):
            for j in range(2):
                packed[i, pl.ds((2 * k + j) * channels, channels)] = filters[9 * i + 3 * j + k]
            packed[i, pl.ds((6 + 2 * k) * channels, channels)] = filters[9 * i + 6 + k]
            packed[i, pl.ds((7 + 2 * k) * channels, channels)] = jnp.zeros((channels, out_channels), BF16)


def conv_pairs(taps, packed, held, padded, plane, part, parts):
    rows = (taps.shape[1] - 1) // parts
    depth, width = taps.shape[2:]
    channels = packed.shape[2]
    total = None
    for i in range(3):
        here = taps[2 * plane + i, pl.ds(part * rows, rows)].reshape(rows * depth, width)
        below = taps[2 * plane + i, pl.ds(part * rows + 1, rows)].reshape(rows * depth, width)
        lhs = jnp.concatenate([here, below], axis=-1)
        term = jnp.dot(lhs, packed[i], preferred_element_type=F32)
        total = term if total is None else total + term
    total = leaky_relu(total).astype(BF16).astype(F32)
    half = rows * depth // 2
    blocks = channels // 128
    for block in range(blocks):
        held[block] = total[:, block * 128 : block * 128 + 128]
    for k in range(2):
        cells = jnp.concatenate([held[block, pl.ds(k, half, stride=2)] for block in range(blocks)], axis=-1)
        pieces = [cells] if k else [cells, shifted_up(cells, depth // 2)]
        for at, piece in zip((k, 2), pieces):
            piece = piece.astype(BF16).reshape(rows // 2, 2, depth // 2, channels)
            for parity in range(2):
                padded[plane, at, parity, pl.ds(part * rows // 2, rows // 2)] = piece[:, parity]


ORDER = (
    ("own", 2), ("home",), ("start",), ("own", 0), ("fold", 1), ("own", 1), ("fold", 2), ("serve", 2, 1),
    ("serve", 0, 1), ("serve", 1, 1), ("hidden", 0, 0), ("serve", 2, 2), ("pass", 2, 1), ("rim",), ("serve", 0,
    2), ("pass", 0, 1), ("hidden", 0, 1), ("serve", 2, 3), ("pass", 1, 1), ("fold", 3), ("serve", 1, 2),
    ("pass", 2, 2), ("serve", 2, 4), ("pass", 0, 2), ("serve", 0, 3), ("pass", 2, 3), ("serve", 1, 3), ("pass",
    1, 2), ("before", 0), ("before", 1), ("serve", 0, 4), ("fold_rim",), ("serve", 1, 4), ("pass", 0, 3),
    ("hidden", 1, 0), ("hidden", 1, 1), ("pass", 1, 3), ("first", 0), ("first", 1),
)


def third_sum(i, lanes, blocks, tap, plane, filters):
    own_rows = filters.shape[2] // 9
    added = None
    for j in range(3):
        for k in range(3):
            rhs = filters[i, pl.ds(lanes, blocks), pl.ds((3 * j + k) * own_rows, own_rows)]
            term = lax.dot_general(
                tap(plane, j, k), rhs.reshape(blocks * own_rows, rhs.shape[2]), (((1,), (1,)), ((), ())),
                preferred_element_type=F32,
            )
            added = term if added is None else added + term
    return added


def ring_kernel(
    volume, first, shard, out,
    cells, first_held, packed, turned, taps, held, padded, filters, total, part_out, part_in,
    local_sem, ring_send, ring_recv, cross_send, cross_recv, side_send, side_recv,
    home_send, home_recv, rim_send, rim_recv,
):
    count = lax.axis_size("chan")
    chips = count // 2
    me = lax.axis_index("chan")
    grp = lax.axis_index("grp")
    core, chip = me % 2, me // 2
    spot = position_of(chip, chips)
    sibling = me + 1 - 2 * core
    right = 2 * chip_at((spot + 1) % chips, chips) + core
    left = 2 * chip_at((spot + chips - 1) % chips, chips) + core
    before, after = (me + count - 1) % count, (me + 1) % count
    planes = volume.shape[0]
    far = chips // 2
    piece = shard.shape[1]
    carried = piece * 10 // 18
    crossed = piece - carried
    halved = piece // 2
    is_first, is_last = me == 0, me == count - 1

    local = [pltpu.make_async_copy(shard, filters.at[:, me], local_sem.at[0])]
    local.append(pltpu.make_async_copy(first, first_held, local_sem.at[1]))
    for plane in range(planes):
        local.append(pltpu.make_async_copy(volume.at[plane], cells.at[plane], local_sem.at[2 + plane]))
    for copy in local[1:3]:
        copy.start()

    barrier = pltpu.get_barrier_semaphore()
    peers = [{"chan": peer} for peer in (left, right, sibling, before, after)] + [{"grp": 1 - grp}]
    for peer in peers:
        pl.semaphore_signal(barrier, inc=1, device_id=peer, device_id_type=pl.DeviceIdType.MESH)
    pl.semaphore_wait(barrier, len(peers))

    def remote(source, target, send, recv, peer):
        return pltpu.make_async_remote_copy(
            src_ref=source, dst_ref=target, send_sem=send, recv_sem=recv,
            device_id=peer, device_id_type=pl.DeviceIdType.MESH,
        )

    def rows_at(offset, size):
        return pl.ds(pl.multiple_of(offset, 16), size)

    def unit_of(way, gone):
        return 2 * chip_at((spot + (chips - gone if way == 0 else gone)) % chips, chips) + core

    def ring_rows(way, gone):
        upper = grp if way == 0 else 1 - grp
        if gone < far:
            return rows_at(upper * crossed, carried)
        return rows_at(upper * halved, halved)

    def ring(way, t, gone):
        unit, rows = unit_of(way, gone - 1), ring_rows(way, gone)
        target = filters.at[t, unit, rows]
        source = shard.at[t, rows] if gone == 1 else target
        return remote(
            source, target, ring_send.at[way, t, gone - 1], ring_recv.at[way, t, gone - 1],
            {"chan": (right, left)[way]},
        )

    def arrival(way, t, gone):
        target = filters.at[t, unit_of(way, gone), ring_rows(way, gone)]
        return remote(
            target, target, ring_send.at[way, t, gone - 1], ring_recv.at[way, t, gone - 1], {"chan": left}
        )

    def cross(way, t, gone):
        upper = grp if way == 0 else 1 - grp
        block = filters.at[t, unit_of(way, gone), rows_at(upper * carried, crossed)]
        at = 2 * (gone - 1) + way
        return remote(block, block, cross_send.at[t, at], cross_recv.at[t, at], {"grp": 1 - grp})

    def side(way, t, gone):
        block = filters.at[t, unit_of(way, gone)]
        return remote(block, block, side_send.at[t], side_recv.at[t], {"chan": sibling})

    home = remote(shard, filters.at[:, me], home_send.at[0], home_recv.at[0], {"chan": sibling})
    rim = remote(volume.at[0], cells.at[planes], rim_send.at[0], rim_recv.at[0], {"chan": before})
    part = remote(part_out, part_in, rim_send.at[1], rim_recv.at[1], {"chan": before})

    for copy in local[3:] + local[:1]:
        copy.start()

    def send_own(t):
        for way in range(2):
            ring(way, t, 1).start()

    def serve(t, gone):
        for way in range(2):
            arrival(way, t, gone).wait_recv()
            if gone < far:
                ring(way, t, gone + 1).start()
                cross(way, t, gone).start()
        if gone == far:
            side(0, t, gone).start()

    def pass_on(t, gone):
        for way in range(2 if gone < far else 0):
            cross(way, t, gone).wait_recv()
            side(way, t, gone).start()

    def all_sides(t):
        block = filters.at[t, pl.ds(0, chips - 1)]
        return remote(block, block, side_send.at[t], side_recv.at[t], {"chan": sibling})

    def all_here(t):
        all_sides(t).wait_recv()

    def all_sent(t):
        for way in range(2):
            for gone in range(1, far + 1):
                ring(way, t, gone).wait_send()
            for gone in range(1, far):
                cross(way, t, gone).wait_send()
        all_sides(t).wait_send()

    tap = tap_reader(padded, padded.shape[3] - 1)
    blocks = filters.shape[1] // 2
    half = blocks * shard.shape[1] // 9
    lanes = [(at * blocks, pl.ds(at * half, half)) for at in range(2)]

    def start_work():
        local[1].wait()
        pack_first(first_held, packed)
        local[2].wait()
        fold_pairs(cells, turned, taps, 0)
        blank = jnp.zeros(padded.shape[4:], BF16)
        for plane in range(planes // 2):
            for k in range(3):
                padded[plane, k, 0, padded.shape[3] - 1] = blank

    def fold_plane(plane):
        local[2 + plane].wait()
        fold_pairs(cells, turned, taps, plane)

    def hidden_part(plane, at):
        conv_pairs(taps, packed, held, padded, plane, at, 2)

    def fold_rim():
        @pl.when(jnp.logical_not(is_last))
        def _():
            rim.wait_recv()

        @pl.when(is_last)
        def _():
            cells[planes] = jnp.zeros(cells.shape[1:], BF16)
            part_in[...] = jnp.zeros(part_in.shape, BF16)

        fold_pairs(cells, turned, taps, planes)

    def send_rim():
        @pl.when(jnp.logical_not(is_first))
        def _():
            rim.start()

    def sum_for_before(at):
        if at == 0:
            home.wait_recv()
            local[0].wait()
            all_here(2)
        first_unit, columns = lanes[at]
        part_out[:, columns] = third_sum(2, first_unit, blocks, tap, 0, filters).astype(BF16)
        if at == 1:
            @pl.when(jnp.logical_not(is_first))
            def _():
                part.start()

    def sum_of_first(at):
        if at == 0:
            all_here(0)
        first_unit, columns = lanes[at]
        total[:, columns] = third_sum(0, first_unit, blocks, tap, 0, filters)

    def sum_of_second():
        @pl.when(jnp.logical_not(is_last))
        def _():
            part.wait_recv()

        all_here(1)
        for at, columns in lanes:
            added = total[:, columns] + part_in[:, columns].astype(F32)
            out[:, columns] = leaky_relu(third_sum(1, at, blocks, tap, 1, filters) + added).astype(BF16)

    actions = {
        "own": send_own, "home": home.start, "start": start_work, "fold": fold_plane, "hidden": hidden_part, "rim": send_rim, "fold_rim": fold_rim,
        "serve": serve, "pass": pass_on, "before": sum_for_before, "first": sum_of_first,
    }
    for name, *at in ORDER:
        actions[name](*at)

    sum_of_second()
    for t in range(3):
        all_sent(t)
    home.wait_send()

    @pl.when(jnp.logical_not(is_first))
    def _():
        rim.wait_send()
        part.wait_send()


def ring_shards(volume, first_filters, second_filters):
    planes, rows, depth, in_channels = volume.shape[1:]
    mid = first_filters.shape[4]
    own = second_filters.shape[4]
    count = lax.axis_size("chan")
    turned_cells = jnp.transpose(volume[0], (0, 1, 3, 2))
    turned_shard = jnp.transpose(second_filters, (0, 1, 2, 4, 3)).reshape(3, 9 * own, mid)
    out_cells = rows // 4 * (depth // 4)
    dma = pltpu.SemaphoreType.DMA
    result = pl.pallas_call(
        ring_kernel,
        out_shape=jax.ShapeDtypeStruct((out_cells, own * count), BF16),
        in_specs=[pl.BlockSpec(memory_space=pl.ANY)] * 3,
        out_specs=whole_vmem(1)[0],
        scratch_shapes=[
            pltpu.VMEM((planes + 1, rows, in_channels, depth), BF16),
            pltpu.VMEM((27, in_channels, mid), BF16),
            pltpu.VMEM((3, 12 * in_channels, mid), BF16),
            pltpu.VMEM((4, depth, 2 * in_channels), F32),
            pltpu.VMEM((planes + 1, rows // 2 + 1, depth // 2, 6 * in_channels), BF16),
            pltpu.VMEM((mid // 128, rows // 4 * (depth // 2), 128), F32),
            pltpu.VMEM((planes // 2, 3, 2, rows // 4 + 1, depth // 4, mid), BF16),
            pltpu.VMEM((3, count, 9 * own, mid), BF16),
            pltpu.VMEM((out_cells, own * count), F32),
            pltpu.VMEM((out_cells, own * count), BF16),
            pltpu.VMEM((out_cells, own * count), BF16),
            dma((2 + planes,)),
            *[dma((2, 3, count // 4))] * 2,
            *[dma((3, count // 2 - 2))] * 2,
            *[dma((3,))] * 2,
            *[dma((1,))] * 2,
            *[dma((2,))] * 2,
        ],
        compiler_params=pltpu.CompilerParams(
            vmem_limit_bytes=VMEM_BYTES, collective_id=0, has_side_effects=True
        ),
    )(turned_cells, first_filters.reshape(27, in_channels, mid), turned_shard)
    return result.reshape(1, planes // 4, rows // 4, depth // 4, own * count)


def shards(volume, first_filters, second_filters):
    fits = lax.axis_size("chan") == 16 and lax.axis_size("grp") == 2
    if fits and second_filters.shape[4] % 32 == 0 and volume.shape[1] == 4:
        return ring_shards(volume, first_filters, second_filters)
    return plain_shards(volume, first_filters, second_filters)


def solution(mesh):
    placed = (P(("grp", "chan"), None, None, None, None), P(), P(None, None, None, None, "chan"))
    return jax.shard_map(
        shards,
        mesh=mesh,
        in_specs=placed,
        out_specs=P(("grp", "chan"), None, None, None, None),
        check_vma=False,
    )
```

```python
import jax
import jax.numpy as jnp
from jax import lax
from jax.experimental import pallas as pl
from jax.experimental.pallas import tpu as pltpu
from jax.sharding import PartitionSpec as P

F32 = jnp.float32
BF16 = jnp.bfloat16
VMEM_BYTES = 56 * 1024 * 1024


def passed_along(value, axis, steps):
    count = lax.axis_size(axis)
    initial, last = (max(0, -steps), min(count, count - steps))
    return lax.ppermute(value, axis, [(source, source + steps) for source in range(initial, last)])


def leaky_relu(values):
    return jnp.where(values > 0, values, 0.3 * values)


def shifted_up(values, period):
    count = values.shape[0]
    moved = pltpu.roll(values, count - 1, 0)
    row = lax.broadcasted_iota(jnp.int32, values.shape, 0)
    return jnp.where(row % period == period - 1, 0.0, moved)


def taps_of_plane(source, source_plane, taps, plane):
    pairs, depth = source.shape[1] // 2, source.shape[2]

    def body(pair, carry):
        for parity in range(2):
            cells = source[source_plane, 2 * pair + parity]
            moved = shifted_up(cells.astype(F32), depth).astype(BF16)
            taps[plane, parity, pair] = jnp.concatenate([cells, moved], axis=-1)
        return carry

    lax.fori_loop(0, pairs, body, 0)


def zero_row(taps, plane):
    taps[plane, 0, taps.shape[2] - 1] = jnp.zeros(taps.shape[3:], BF16)


def conv_first(taps, filters, held, hidden, plane, part, parts):
    rows = hidden.shape[3] * 2 // parts
    depth, width = taps.shape[3:]
    total = None
    for i in range(3):
        for j in range(3):
            lhs = taps[2 * plane + i, j % 2, pl.ds(part * rows + j // 2, rows)]
            term = jnp.dot(lhs.reshape(rows * depth, width), filters[3 * i + j], preferred_element_type=F32)
            total = term if total is None else total + term
    total = leaky_relu(total).astype(BF16).astype(F32)
    half = rows * depth // 2
    channels = hidden.shape[5]
    blocks = channels // 128
    for block in range(blocks):
        held[block] = total[:, block * 128 : block * 128 + 128]
    for k in range(2):
        cells = jnp.concatenate([held[block, pl.ds(k, half, stride=2)] for block in range(blocks)], axis=-1)
        pieces = [cells] if k else [cells, shifted_up(cells, depth // 2)]
        for at, piece in zip((k, 2), pieces):
            piece = piece.astype(BF16).reshape(rows // 2, 2, depth // 2, channels)
            for parity in range(2):
                hidden[plane, at, parity, pl.ds(part * rows // 2, rows // 2)] = piece[:, parity]


def conv_second(tap, filters, out):
    width = 256 if out.shape[1] % 256 == 0 else out.shape[1]
    for at in range(out.shape[1] // width):
        total = None
        for i in range(3):
            for j in range(3):
                for k in range(3):
                    rhs = filters[9 * i + 3 * j + k, pl.ds(at * width, width)]
                    term = lax.dot_general(
                        tap(i, j, k), rhs, (((1,), (1,)), ((), ())), preferred_element_type=F32
                    )
                    total = term if total is None else total + term
        out[:, pl.ds(at * width, width)] = leaky_relu(total).astype(BF16)


def first_kernel(cells, rim, filters, hidden, taps, held):
    planes = cells.shape[0]
    for plane in range(planes + 1):
        taps_of_plane(cells if plane < planes else rim, plane % planes, taps, plane)
        zero_row(taps, plane)
    for plane in range(planes // 2):
        for part in range(2):
            conv_first(taps, filters, held, hidden, plane, part, 2)


def padded_rows(hidden, rim, padded):
    planes = hidden.shape[0]
    rows = hidden.shape[3]
    for plane in range(planes + 1):
        for k in range(3):
            padded[plane, k, :, pl.ds(0, rows)] = hidden[plane, k] if plane < planes else rim[0, k]
            padded[plane, k, 0, rows] = jnp.zeros(padded.shape[4:], BF16)


def tap_reader(padded, rows):
    depth, channels = padded.shape[4:]

    def tap(i, j, k):
        return padded[i, k, j % 2, pl.ds(j // 2, rows)].reshape(rows * depth, channels)

    return tap


def second_kernel(hidden, rim, filters, out, padded):
    padded_rows(hidden, rim, padded)
    conv_second(tap_reader(padded, hidden.shape[3]), filters, out)


def whole_vmem(count):
    return [pl.BlockSpec(memory_space=pltpu.VMEM)] * count


def padded_first(first_filters):
    kernel, in_channels, out_channels = first_filters.shape[2:]
    flat = first_filters.reshape(9, kernel * in_channels, out_channels)
    return jnp.pad(flat, ((0, 0), (0, in_channels), (0, 0)))


def plain_shards(volume, first_filters, second_filters):
    planes, rows, depth, in_channels = volume.shape[1:]
    mid = first_filters.shape[4]
    turned = jnp.transpose(second_filters, (0, 1, 2, 4, 3)).reshape(27, second_filters.shape[4], mid)
    gathered = lax.all_gather(turned, "chan", axis=1, tiled=True)
    cells = volume.reshape(planes, rows, depth // 2, 2 * in_channels)
    rim = passed_along(cells[:1], "chan", -1)
    filters = padded_first(first_filters)
    hidden_shape = (planes // 2, 3, 2, rows // 4, depth // 4, mid)
    hidden = pl.pallas_call(
        first_kernel,
        out_shape=jax.ShapeDtypeStruct(hidden_shape, BF16),
        in_specs=whole_vmem(3),
        out_specs=whole_vmem(1)[0],
        scratch_shapes=[
            pltpu.VMEM((planes + 1, 2, rows // 2 + 1, depth // 2, 4 * in_channels), BF16),
            pltpu.VMEM((mid // 128, rows // 4 * (depth // 2), 128), F32),
        ],
        compiler_params=pltpu.CompilerParams(vmem_limit_bytes=VMEM_BYTES),
    )(cells, rim, filters)
    hidden_rim = passed_along(hidden[:1], "chan", -1)
    out_cells = rows // 4 * (depth // 4)
    out_channels = gathered.shape[1]
    result = pl.pallas_call(
        second_kernel,
        out_shape=jax.ShapeDtypeStruct((out_cells, out_channels), BF16),
        in_specs=whole_vmem(3),
        out_specs=whole_vmem(1)[0],
        scratch_shapes=[
            pltpu.VMEM((planes // 2 + 1, 3, 2, rows // 4 + 1, depth // 4, mid), BF16),
        ],
        compiler_params=pltpu.CompilerParams(vmem_limit_bytes=VMEM_BYTES),
    )(hidden, hidden_rim, gathered)
    return result.reshape(1, planes // 4, rows // 4, depth // 4, out_channels)


def position_of(chip, chips):
    column, along = chip % 2, chip // 2
    return along * (1 - column) + (chips - 1 - along) * column


def chip_at(position, chips):
    upper = position // (chips // 2)
    return (1 - upper) * 2 * position + upper * (2 * (chips - 1 - position) + 1)


def fold_pairs(cells, turned, taps, plane):
    pairs = cells.shape[1] // 2
    channels, depth = cells.shape[2:]
    slots = turned.shape[0]

    def body(step, carry):
        for slot in range(slots):
            pair = step * slots + slot
            both = cells[plane, pl.ds(2 * pair, 2)].reshape(2 * channels, depth)
            turned[slot] = both.astype(F32).T
            even = turned[slot, pl.ds(0, depth // 2, stride=2)]
            odd = turned[slot, pl.ds(1, depth // 2, stride=2)]
            later = shifted_up(even, depth // 2)
            taps[plane, pair] = jnp.concatenate([even, odd, later], axis=-1).astype(BF16)
        return carry

    lax.fori_loop(0, pairs // slots, body, 0)
    taps[plane, pairs] = jnp.zeros(taps.shape[2:], BF16)


def pack_first(filters, packed):
    channels, out_channels = filters.shape[1:]
    for i in range(3):
        for k in range(3):
            for j in range(2):
                packed[i, pl.ds((2 * k + j) * channels, channels)] = filters[9 * i + 3 * j + k]
            packed[i, pl.ds((6 + 2 * k) * channels, channels)] = filters[9 * i + 6 + k]
            packed[i, pl.ds((7 + 2 * k) * channels, channels)] = jnp.zeros((channels, out_channels), BF16)


def pair_sum(taps, packed, plane, part, parts, offsets):
    rows = (taps.shape[1] - 1) // parts
    depth, width = taps.shape[2:]
    total = None
    for i in offsets:
        here = taps[2 * plane + i, pl.ds(part * rows, rows)].reshape(rows * depth, width)
        below = taps[2 * plane + i, pl.ds(part * rows + 1, rows)].reshape(rows * depth, width)
        lhs = jnp.concatenate([here, below], axis=-1)
        term = jnp.dot(lhs, packed[i], preferred_element_type=F32)
        total = term if total is None else total + term
    return total


def store_hidden(total, held, padded, plane, part, parts):
    depth = 2 * padded.shape[4]
    rows = total.shape[0] // depth
    channels = total.shape[1]
    total = leaky_relu(total).astype(BF16).astype(F32)
    half = rows * depth // 2
    blocks = channels // 128
    for block in range(blocks):
        held[block] = total[:, block * 128 : block * 128 + 128]
    for k in range(2):
        cells = jnp.concatenate([held[block, pl.ds(k, half, stride=2)] for block in range(blocks)], axis=-1)
        pieces = [cells] if k else [cells, shifted_up(cells, depth // 2)]
        for at, piece in zip((k, 2), pieces):
            piece = piece.astype(BF16).reshape(rows // 2, 2, depth // 2, channels)
            for parity in range(2):
                padded[plane, at, parity, pl.ds(part * rows // 2, rows // 2)] = piece[:, parity]


ORDER = (
    ("own", 2), ("home",), ("start",), ("own", 0), ("fold", 1), ("own", 1), ("fold", 2), ("serve", 2, 1),
    ("serve", 0, 1), ("serve", 1, 1), ("hidden", 0, 0), ("serve", 2, 2), ("pass", 2, 1), ("rim",), ("serve", 0,
    2), ("pass", 0, 1), ("hidden", 0, 1), ("serve", 2, 3), ("pass", 1, 1), ("fold", 3), ("early", 0), ("serve",
    1, 2), ("pass", 2, 2), ("early", 1), ("serve", 2, 4), ("pass", 0, 2), ("serve", 0, 3), ("pass", 2, 3),
    ("serve", 1, 3), ("pass", 1, 2), ("before", 0), ("before", 1), ("serve", 0, 4), ("fold_rim",), ("serve", 1,
    4), ("pass", 0, 3), ("hidden", 1, 0), ("hidden", 1, 1), ("pass", 1, 3), ("first", 0), ("first", 1),
)


def third_sum(i, lanes, blocks, tap, plane, filters):
    own_rows = filters.shape[2] // 9
    added = None
    for j in range(3):
        for k in range(3):
            rhs = filters[i, pl.ds(lanes, blocks), pl.ds((3 * j + k) * own_rows, own_rows)]
            term = lax.dot_general(
                tap(plane, j, k), rhs.reshape(blocks * own_rows, rhs.shape[2]), (((1,), (1,)), ((), ())),
                preferred_element_type=F32,
            )
            added = term if added is None else added + term
    return added


def ring_kernel(
    volume, first, shard, out,
    cells, first_held, packed, turned, taps, held, padded, filters, total, early, part_out, part_in,
    local_sem, ring_send, ring_recv, cross_send, cross_recv, side_send, side_recv,
    home_send, home_recv, rim_send, rim_recv,
):
    count = lax.axis_size("chan")
    chips = count // 2
    me = lax.axis_index("chan")
    grp = lax.axis_index("grp")
    core, chip = me % 2, me // 2
    spot = position_of(chip, chips)
    sibling = me + 1 - 2 * core
    right = 2 * chip_at((spot + 1) % chips, chips) + core
    left = 2 * chip_at((spot + chips - 1) % chips, chips) + core
    before, after = (me + count - 1) % count, (me + 1) % count
    planes = volume.shape[0]
    far = chips // 2
    piece = shard.shape[1]
    carried = piece * 10 // 18
    crossed = piece - carried
    halves = (160, piece - 160)
    is_first, is_last = me == 0, me == count - 1

    local = [pltpu.make_async_copy(shard, filters.at[:, me], local_sem.at[0])]
    local.append(pltpu.make_async_copy(first, first_held, local_sem.at[1]))
    for plane in range(planes):
        local.append(pltpu.make_async_copy(volume.at[plane], cells.at[plane], local_sem.at[2 + plane]))
    for copy in local[1:3]:
        copy.start()

    barrier = pltpu.get_barrier_semaphore()
    peers = [{"chan": peer} for peer in (left, right, sibling, before, after)] + [{"grp": 1 - grp}]
    for peer in peers:
        pl.semaphore_signal(barrier, inc=1, device_id=peer, device_id_type=pl.DeviceIdType.MESH)
    pl.semaphore_wait(barrier, len(peers))

    def remote(source, target, send, recv, peer):
        return pltpu.make_async_remote_copy(
            src_ref=source, dst_ref=target, send_sem=send, recv_sem=recv,
            device_id=peer, device_id_type=pl.DeviceIdType.MESH,
        )

    def rows_at(offset, size):
        return pl.ds(pl.multiple_of(offset, 16), size)

    def unit_of(way, gone):
        return 2 * chip_at((spot + (chips - gone if way == 0 else gone)) % chips, chips) + core

    def ring_rows(way, gone):
        upper = grp if way == 0 else 1 - grp
        if gone < far:
            return rows_at(upper * crossed, carried)
        return rows_at(upper * (piece - halves[way]), halves[way])

    def ring(way, t, gone):
        unit, rows = unit_of(way, gone - 1), ring_rows(way, gone)
        target = filters.at[t, unit, rows]
        source = shard.at[t, rows] if gone == 1 else target
        return remote(
            source, target, ring_send.at[way, t, gone - 1], ring_recv.at[way, t, gone - 1],
            {"chan": (right, left)[way]},
        )

    def arrival(way, t, gone):
        target = filters.at[t, unit_of(way, gone), ring_rows(way, gone)]
        return remote(
            target, target, ring_send.at[way, t, gone - 1], ring_recv.at[way, t, gone - 1], {"chan": left}
        )

    def cross(way, t, gone):
        upper = grp if way == 0 else 1 - grp
        block = filters.at[t, unit_of(way, gone), rows_at(upper * carried, crossed)]
        at = 2 * (gone - 1) + way
        return remote(block, block, cross_send.at[t, at], cross_recv.at[t, at], {"grp": 1 - grp})

    def side(way, t, gone):
        block = filters.at[t, unit_of(way, gone)]
        return remote(block, block, side_send.at[t], side_recv.at[t], {"chan": sibling})

    home = remote(shard, filters.at[:, me], home_send.at[0], home_recv.at[0], {"chan": sibling})
    rim = remote(volume.at[0], cells.at[planes], rim_send.at[0], rim_recv.at[0], {"chan": before})
    part = remote(part_out, part_in, rim_send.at[1], rim_recv.at[1], {"chan": before})

    for copy in local[3:] + local[:1]:
        copy.start()

    def send_own(t):
        for way in range(2):
            ring(way, t, 1).start()

    def serve(t, gone):
        for way in (1, 0):
            arrival(way, t, gone).wait_recv()
            if gone < far:
                ring(way, t, gone + 1).start()
                cross(way, t, gone).start()
        if gone == far:
            side(0, t, gone).start()

    def pass_on(t, gone):
        for way in range(2 if gone < far else 0):
            cross(way, t, gone).wait_recv()
            side(way, t, gone).start()

    def all_sides(t):
        block = filters.at[t, pl.ds(0, chips - 1)]
        return remote(block, block, side_send.at[t], side_recv.at[t], {"chan": sibling})

    def all_here(t):
        all_sides(t).wait_recv()

    def all_sent(t):
        for way in range(2):
            for gone in range(1, far + 1):
                ring(way, t, gone).wait_send()
            for gone in range(1, far):
                cross(way, t, gone).wait_send()
        all_sides(t).wait_send()

    tap = tap_reader(padded, padded.shape[3] - 1)
    blocks = filters.shape[1] // 2
    half = blocks * shard.shape[1] // 9
    lanes = [(at * blocks, pl.ds(at * half, half)) for at in range(2)]

    def start_work():
        local[1].wait()
        pack_first(first_held, packed)
        local[2].wait()
        fold_pairs(cells, turned, taps, 0)
        blank = jnp.zeros(padded.shape[4:], BF16)
        for plane in range(planes // 2):
            for k in range(3):
                padded[plane, k, 0, padded.shape[3] - 1] = blank

    def fold_plane(plane):
        local[2 + plane].wait()
        fold_pairs(cells, turned, taps, plane)

    def hidden_part(plane, at):
        if plane == 0:
            added = pair_sum(taps, packed, plane, at, 2, range(3))
        else:
            added = early[at] + pair_sum(taps, packed, plane, at, 2, (2,))
        store_hidden(added, held, padded, plane, at, 2)

    def early_sum(at):
        early[at] = pair_sum(taps, packed, 1, at, 2, range(2))

    def fold_rim():
        @pl.when(jnp.logical_not(is_last))
        def _():
            rim.wait_recv()

        @pl.when(is_last)
        def _():
            cells[planes] = jnp.zeros(cells.shape[1:], BF16)
            part_in[...] = jnp.zeros(part_in.shape, BF16)

        fold_pairs(cells, turned, taps, planes)

    def send_rim():
        @pl.when(jnp.logical_not(is_first))
        def _():
            rim.start()

    def sum_for_before(at):
        if at == 0:
            home.wait_recv()
            local[0].wait()
            all_here(2)
        first_unit, columns = lanes[at]
        part_out[:, columns] = third_sum(2, first_unit, blocks, tap, 0, filters).astype(BF16)
        if at == 1:
            @pl.when(jnp.logical_not(is_first))
            def _():
                part.start()

    def sum_of_first(at):
        if at == 0:
            all_here(0)
        first_unit, columns = lanes[at]
        total[:, columns] = third_sum(0, first_unit, blocks, tap, 0, filters)

    def sum_of_second():
        @pl.when(jnp.logical_not(is_last))
        def _():
            part.wait_recv()

        all_here(1)
        for at, columns in lanes:
            added = total[:, columns] + part_in[:, columns].astype(F32)
            out[:, columns] = leaky_relu(third_sum(1, at, blocks, tap, 1, filters) + added).astype(BF16)

    actions = {
        "own": send_own, "home": home.start, "start": start_work, "fold": fold_plane, "hidden": hidden_part, "early": early_sum, "rim": send_rim, "fold_rim": fold_rim,
        "serve": serve, "pass": pass_on, "before": sum_for_before, "first": sum_of_first,
    }
    for name, *at in ORDER:
        actions[name](*at)

    sum_of_second()
    for t in range(3):
        all_sent(t)
    home.wait_send()

    @pl.when(jnp.logical_not(is_first))
    def _():
        rim.wait_send()
        part.wait_send()


def ring_shards(volume, first_filters, second_filters):
    planes, rows, depth, in_channels = volume.shape[1:]
    mid = first_filters.shape[4]
    own = second_filters.shape[4]
    count = lax.axis_size("chan")
    turned_cells = jnp.transpose(volume[0], (0, 1, 3, 2))
    turned_shard = jnp.transpose(second_filters, (0, 1, 2, 4, 3)).reshape(3, 9 * own, mid)
    out_cells = rows // 4 * (depth // 4)
    dma = pltpu.SemaphoreType.DMA
    result = pl.pallas_call(
        ring_kernel,
        out_shape=jax.ShapeDtypeStruct((out_cells, own * count), BF16),
        in_specs=[pl.BlockSpec(memory_space=pl.ANY)] * 3,
        out_specs=whole_vmem(1)[0],
        scratch_shapes=[
            pltpu.VMEM((planes + 1, rows, in_channels, depth), BF16),
            pltpu.VMEM((27, in_channels, mid), BF16),
            pltpu.VMEM((3, 12 * in_channels, mid), BF16),
            pltpu.VMEM((4, depth, 2 * in_channels), F32),
            pltpu.VMEM((planes + 1, rows // 2 + 1, depth // 2, 6 * in_channels), BF16),
            pltpu.VMEM((mid // 128, rows // 4 * (depth // 2), 128), F32),
            pltpu.VMEM((planes // 2, 3, 2, rows // 4 + 1, depth // 4, mid), BF16),
            pltpu.VMEM((3, count, 9 * own, mid), BF16),
            pltpu.VMEM((out_cells, own * count), F32),
            pltpu.VMEM((2, rows // 4 * (depth // 2), mid), F32),
            pltpu.VMEM((out_cells, own * count), BF16),
            pltpu.VMEM((out_cells, own * count), BF16),
            dma((2 + planes,)),
            *[dma((2, 3, count // 4))] * 2,
            *[dma((3, count // 2 - 2))] * 2,
            *[dma((3,))] * 2,
            *[dma((1,))] * 2,
            *[dma((2,))] * 2,
        ],
        compiler_params=pltpu.CompilerParams(
            vmem_limit_bytes=VMEM_BYTES, collective_id=0, has_side_effects=True
        ),
    )(turned_cells, first_filters.reshape(27, in_channels, mid), turned_shard)
    return result.reshape(1, planes // 4, rows // 4, depth // 4, own * count)


def shards(volume, first_filters, second_filters):
    fits = lax.axis_size("chan") == 16 and lax.axis_size("grp") == 2
    if fits and second_filters.shape[4] % 32 == 0 and volume.shape[1] == 4:
        return ring_shards(volume, first_filters, second_filters)
    return plain_shards(volume, first_filters, second_filters)


def solution(mesh):
    placed = (P(("grp", "chan"), None, None, None, None), P(), P(None, None, None, None, "chan"))
    return jax.shard_map(
        shards,
        mesh=mesh,
        in_specs=placed,
        out_specs=P(("grp", "chan"), None, None, None, None),
        check_vma=False,
    )
```

```python
import jax
import jax.numpy as jnp
from jax import lax
from jax.experimental import pallas as pl
from jax.experimental.pallas import tpu as pltpu
from jax.sharding import PartitionSpec as P

F32 = jnp.float32
BF16 = jnp.bfloat16
VMEM_BYTES = 56 * 1024 * 1024


def passed_along(value, axis, steps):
    count = lax.axis_size(axis)
    initial, last = (max(0, -steps), min(count, count - steps))
    return lax.ppermute(value, axis, [(source, source + steps) for source in range(initial, last)])


def leaky_relu(values):
    return jnp.where(values > 0, values, 0.3 * values)


def shifted_up(values, period):
    count = values.shape[0]
    moved = pltpu.roll(values, count - 1, 0)
    row = lax.broadcasted_iota(jnp.int32, values.shape, 0)
    return jnp.where(row % period == period - 1, 0.0, moved)


def taps_of_plane(source, source_plane, taps, plane):
    pairs, depth = source.shape[1] // 2, source.shape[2]

    def body(pair, carry):
        for parity in range(2):
            cells = source[source_plane, 2 * pair + parity]
            moved = shifted_up(cells.astype(F32), depth).astype(BF16)
            taps[plane, parity, pair] = jnp.concatenate([cells, moved], axis=-1)
        return carry

    lax.fori_loop(0, pairs, body, 0)


def zero_row(taps, plane):
    taps[plane, 0, taps.shape[2] - 1] = jnp.zeros(taps.shape[3:], BF16)


def conv_first(taps, filters, held, hidden, plane, part, parts):
    rows = hidden.shape[3] * 2 // parts
    depth, width = taps.shape[3:]
    total = None
    for i in range(3):
        for j in range(3):
            lhs = taps[2 * plane + i, j % 2, pl.ds(part * rows + j // 2, rows)]
            term = jnp.dot(lhs.reshape(rows * depth, width), filters[3 * i + j], preferred_element_type=F32)
            total = term if total is None else total + term
    total = leaky_relu(total).astype(BF16).astype(F32)
    half = rows * depth // 2
    channels = hidden.shape[5]
    blocks = channels // 128
    for block in range(blocks):
        held[block] = total[:, block * 128 : block * 128 + 128]
    for k in range(2):
        cells = jnp.concatenate([held[block, pl.ds(k, half, stride=2)] for block in range(blocks)], axis=-1)
        pieces = [cells] if k else [cells, shifted_up(cells, depth // 2)]
        for at, piece in zip((k, 2), pieces):
            piece = piece.astype(BF16).reshape(rows // 2, 2, depth // 2, channels)
            for parity in range(2):
                hidden[plane, at, parity, pl.ds(part * rows // 2, rows // 2)] = piece[:, parity]


def conv_second(tap, filters, out):
    width = 256 if out.shape[1] % 256 == 0 else out.shape[1]
    for at in range(out.shape[1] // width):
        total = None
        for i in range(3):
            for j in range(3):
                for k in range(3):
                    rhs = filters[9 * i + 3 * j + k, pl.ds(at * width, width)]
                    term = lax.dot_general(
                        tap(i, j, k), rhs, (((1,), (1,)), ((), ())), preferred_element_type=F32
                    )
                    total = term if total is None else total + term
        out[:, pl.ds(at * width, width)] = leaky_relu(total).astype(BF16)


def first_kernel(cells, rim, filters, hidden, taps, held):
    planes = cells.shape[0]
    for plane in range(planes + 1):
        taps_of_plane(cells if plane < planes else rim, plane % planes, taps, plane)
        zero_row(taps, plane)
    for plane in range(planes // 2):
        for part in range(2):
            conv_first(taps, filters, held, hidden, plane, part, 2)


def padded_rows(hidden, rim, padded):
    planes = hidden.shape[0]
    rows = hidden.shape[3]
    for plane in range(planes + 1):
        for k in range(3):
            padded[plane, k, :, pl.ds(0, rows)] = hidden[plane, k] if plane < planes else rim[0, k]
            padded[plane, k, 0, rows] = jnp.zeros(padded.shape[4:], BF16)


def tap_reader(padded, rows):
    depth, channels = padded.shape[4:]

    def tap(i, j, k):
        return padded[i, k, j % 2, pl.ds(j // 2, rows)].reshape(rows * depth, channels)

    return tap


def second_kernel(hidden, rim, filters, out, padded):
    padded_rows(hidden, rim, padded)
    conv_second(tap_reader(padded, hidden.shape[3]), filters, out)


def whole_vmem(count):
    return [pl.BlockSpec(memory_space=pltpu.VMEM)] * count


def padded_first(first_filters):
    kernel, in_channels, out_channels = first_filters.shape[2:]
    flat = first_filters.reshape(9, kernel * in_channels, out_channels)
    return jnp.pad(flat, ((0, 0), (0, in_channels), (0, 0)))


def plain_shards(volume, first_filters, second_filters):
    planes, rows, depth, in_channels = volume.shape[1:]
    mid = first_filters.shape[4]
    turned = jnp.transpose(second_filters, (0, 1, 2, 4, 3)).reshape(27, second_filters.shape[4], mid)
    gathered = lax.all_gather(turned, "chan", axis=1, tiled=True)
    cells = volume.reshape(planes, rows, depth // 2, 2 * in_channels)
    rim = passed_along(cells[:1], "chan", -1)
    filters = padded_first(first_filters)
    hidden_shape = (planes // 2, 3, 2, rows // 4, depth // 4, mid)
    hidden = pl.pallas_call(
        first_kernel,
        out_shape=jax.ShapeDtypeStruct(hidden_shape, BF16),
        in_specs=whole_vmem(3),
        out_specs=whole_vmem(1)[0],
        scratch_shapes=[
            pltpu.VMEM((planes + 1, 2, rows // 2 + 1, depth // 2, 4 * in_channels), BF16),
            pltpu.VMEM((mid // 128, rows // 4 * (depth // 2), 128), F32),
        ],
        compiler_params=pltpu.CompilerParams(vmem_limit_bytes=VMEM_BYTES),
    )(cells, rim, filters)
    hidden_rim = passed_along(hidden[:1], "chan", -1)
    out_cells = rows // 4 * (depth // 4)
    out_channels = gathered.shape[1]
    result = pl.pallas_call(
        second_kernel,
        out_shape=jax.ShapeDtypeStruct((out_cells, out_channels), BF16),
        in_specs=whole_vmem(3),
        out_specs=whole_vmem(1)[0],
        scratch_shapes=[
            pltpu.VMEM((planes // 2 + 1, 3, 2, rows // 4 + 1, depth // 4, mid), BF16),
        ],
        compiler_params=pltpu.CompilerParams(vmem_limit_bytes=VMEM_BYTES),
    )(hidden, hidden_rim, gathered)
    return result.reshape(1, planes // 4, rows // 4, depth // 4, out_channels)


def position_of(chip, chips):
    column, along = chip % 2, chip // 2
    return along * (1 - column) + (chips - 1 - along) * column


def chip_at(position, chips):
    upper = position // (chips // 2)
    return (1 - upper) * 2 * position + upper * (2 * (chips - 1 - position) + 1)


def fold_pairs(cells, turned, taps, plane):
    pairs = cells.shape[1] // 2
    channels, depth = cells.shape[2:]
    slots = turned.shape[0]

    def body(step, carry):
        for slot in range(slots):
            pair = step * slots + slot
            both = cells[plane, pl.ds(2 * pair, 2)].reshape(2 * channels, depth)
            turned[slot] = both.astype(F32).T
            even = turned[slot, pl.ds(0, depth // 2, stride=2)]
            odd = turned[slot, pl.ds(1, depth // 2, stride=2)]
            later = shifted_up(even, depth // 2)
            taps[plane, pair] = jnp.concatenate([even, odd, later], axis=-1).astype(BF16)
        return carry

    lax.fori_loop(0, pairs // slots, body, 0)
    taps[plane, pairs] = jnp.zeros(taps.shape[2:], BF16)


def pack_first(filters, packed):
    channels, out_channels = filters.shape[1:]
    for i in range(3):
        for k in range(3):
            for j in range(2):
                packed[i, pl.ds((2 * k + j) * channels, channels)] = filters[9 * i + 3 * j + k]
            packed[i, pl.ds((6 + 2 * k) * channels, channels)] = filters[9 * i + 6 + k]
            packed[i, pl.ds((7 + 2 * k) * channels, channels)] = jnp.zeros((channels, out_channels), BF16)


def pair_sum(taps, packed, plane, part, parts, offsets):
    rows = (taps.shape[1] - 1) // parts
    depth, width = taps.shape[2:]
    total = None
    for i in offsets:
        here = taps[2 * plane + i, pl.ds(part * rows, rows)].reshape(rows * depth, width)
        below = taps[2 * plane + i, pl.ds(part * rows + 1, rows)].reshape(rows * depth, width)
        lhs = jnp.concatenate([here, below], axis=-1)
        term = jnp.dot(lhs, packed[i], preferred_element_type=F32)
        total = term if total is None else total + term
    return total


def store_hidden(total, held, padded, plane, part, parts):
    depth = 2 * padded.shape[4]
    rows = total.shape[0] // depth
    channels = total.shape[1]
    total = leaky_relu(total).astype(BF16).astype(F32)
    half = rows * depth // 2
    blocks = channels // 128
    for block in range(blocks):
        held[block] = total[:, block * 128 : block * 128 + 128]
    for k in range(2):
        cells = jnp.concatenate([held[block, pl.ds(k, half, stride=2)] for block in range(blocks)], axis=-1)
        pieces = [cells] if k else [cells, shifted_up(cells, depth // 2)]
        for at, piece in zip((k, 2), pieces):
            piece = piece.astype(BF16).reshape(rows // 2, 2, depth // 2, channels)
            for parity in range(2):
                padded[plane, at, parity, pl.ds(part * rows // 2, rows // 2)] = piece[:, parity]


ORDER = (
    ("own", 2), ("home",), ("start",), ("own", 0), ("fold", 1), ("own", 1), ("fold", 2), ("serve", 2, 1),
    ("serve", 0, 1), ("serve", 1, 1), ("hidden", 0, 0), ("serve", 2, 2), ("pass", 2, 1), ("rim",), ("serve", 0,
    2), ("pass", 0, 1), ("hidden", 0, 1), ("serve", 2, 3), ("pass", 1, 1), ("fold", 3), ("early", 0), ("serve",
    1, 2), ("pass", 2, 2), ("early", 1), ("serve", 2, 4), ("pass", 0, 2), ("serve", 0, 3), ("pass", 2, 3),
    ("serve", 1, 3), ("before", 0), ("before", 1), ("pass", 1, 2), ("serve", 0, 4), ("fold_rim",), ("serve", 1,
    4), ("sent", 2), ("pass", 0, 3), ("hidden", 1, 0), ("hidden", 1, 1), ("pass", 1, 3), ("first", 0), ("first",
    1), ("sent", 0), ("rims_sent",),
)


def third_sum(i, lanes, blocks, tap, plane, filters):
    own_rows = filters.shape[2] // 9
    added = None
    for j in range(3):
        for k in range(3):
            rhs = filters[i, pl.ds(lanes, blocks), pl.ds((3 * j + k) * own_rows, own_rows)]
            term = lax.dot_general(
                tap(plane, j, k), rhs.reshape(blocks * own_rows, rhs.shape[2]), (((1,), (1,)), ((), ())),
                preferred_element_type=F32,
            )
            added = term if added is None else added + term
    return added


def ring_kernel(
    volume, first, shard, out,
    cells, first_held, packed, turned, taps, held, padded, filters, total, early, part_out, part_in,
    local_sem, ring_send, ring_recv, cross_send, cross_recv, side_send, side_recv,
    home_send, home_recv, rim_send, rim_recv,
):
    count = lax.axis_size("chan")
    chips = count // 2
    me = lax.axis_index("chan")
    grp = lax.axis_index("grp")
    core, chip = me % 2, me // 2
    spot = position_of(chip, chips)
    sibling = me + 1 - 2 * core
    right = 2 * chip_at((spot + 1) % chips, chips) + core
    left = 2 * chip_at((spot + chips - 1) % chips, chips) + core
    before, after = (me + count - 1) % count, (me + 1) % count
    planes = volume.shape[0]
    far = chips // 2
    piece = shard.shape[1]
    carried = piece * 10 // 18
    crossed = piece - carried
    halves = (160, piece - 160)
    is_first, is_last = me == 0, me == count - 1

    local = [pltpu.make_async_copy(shard, filters.at[:, me], local_sem.at[0])]
    local.append(pltpu.make_async_copy(first, first_held, local_sem.at[1]))
    for plane in range(planes):
        local.append(pltpu.make_async_copy(volume.at[plane], cells.at[plane], local_sem.at[2 + plane]))
    for copy in local[1:3]:
        copy.start()

    barrier = pltpu.get_barrier_semaphore()
    peers = [{"chan": peer} for peer in (left, right, sibling, before, after)] + [{"grp": 1 - grp}]
    for peer in peers:
        pl.semaphore_signal(barrier, inc=1, device_id=peer, device_id_type=pl.DeviceIdType.MESH)
    pl.semaphore_wait(barrier, len(peers))

    def remote(source, target, send, recv, peer):
        return pltpu.make_async_remote_copy(
            src_ref=source, dst_ref=target, send_sem=send, recv_sem=recv,
            device_id=peer, device_id_type=pl.DeviceIdType.MESH,
        )

    def rows_at(offset, size):
        return pl.ds(pl.multiple_of(offset, 16), size)

    def unit_of(way, gone):
        return 2 * chip_at((spot + (chips - gone if way == 0 else gone)) % chips, chips) + core

    def ring_rows(way, gone):
        upper = grp if way == 0 else 1 - grp
        if gone < far:
            return rows_at(upper * crossed, carried)
        return rows_at(upper * (piece - halves[way]), halves[way])

    def ring(way, t, gone):
        unit, rows = unit_of(way, gone - 1), ring_rows(way, gone)
        target = filters.at[t, unit, rows]
        source = shard.at[t, rows] if gone == 1 else target
        return remote(
            source, target, ring_send.at[way, t, gone - 1], ring_recv.at[way, t, gone - 1],
            {"chan": (right, left)[way]},
        )

    def arrival(way, t, gone):
        target = filters.at[t, unit_of(way, gone), ring_rows(way, gone)]
        return remote(
            target, target, ring_send.at[way, t, gone - 1], ring_recv.at[way, t, gone - 1], {"chan": left}
        )

    def cross(way, t, gone):
        upper = grp if way == 0 else 1 - grp
        block = filters.at[t, unit_of(way, gone), rows_at(upper * carried, crossed)]
        at = 2 * (gone - 1) + way
        return remote(block, block, cross_send.at[t, at], cross_recv.at[t, at], {"grp": 1 - grp})

    def side(way, t, gone):
        block = filters.at[t, unit_of(way, gone)]
        return remote(block, block, side_send.at[t], side_recv.at[t], {"chan": sibling})

    home = remote(shard, filters.at[:, me], home_send.at[0], home_recv.at[0], {"chan": sibling})
    rim = remote(volume.at[0], cells.at[planes], rim_send.at[0], rim_recv.at[0], {"chan": before})
    part = remote(part_out, part_in, rim_send.at[1], rim_recv.at[1], {"chan": before})

    for copy in local[3:] + local[:1]:
        copy.start()

    def send_own(t):
        for way in range(2):
            ring(way, t, 1).start()

    def serve(t, gone):
        for way in (1, 0):
            arrival(way, t, gone).wait_recv()
            if gone < far:
                ring(way, t, gone + 1).start()
                cross(way, t, gone).start()
        if gone == far:
            side(0, t, gone).start()

    def pass_on(t, gone):
        for way in range(2 if gone < far else 0):
            cross(way, t, gone).wait_recv()
            side(way, t, gone).start()

    def all_sides(t):
        block = filters.at[t, pl.ds(0, chips - 1)]
        return remote(block, block, side_send.at[t], side_recv.at[t], {"chan": sibling})

    def all_here(t):
        all_sides(t).wait_recv()

    def all_sent(t):
        for way in range(2):
            for gone in range(1, far + 1):
                ring(way, t, gone).wait_send()
            for gone in range(1, far):
                cross(way, t, gone).wait_send()
        all_sides(t).wait_send()

    tap = tap_reader(padded, padded.shape[3] - 1)
    blocks = filters.shape[1] // 2
    half = blocks * shard.shape[1] // 9
    lanes = [(at * blocks, pl.ds(at * half, half)) for at in range(2)]

    def start_work():
        local[1].wait()
        pack_first(first_held, packed)
        local[2].wait()
        fold_pairs(cells, turned, taps, 0)
        blank = jnp.zeros(padded.shape[4:], BF16)
        for plane in range(planes // 2):
            for k in range(3):
                padded[plane, k, 0, padded.shape[3] - 1] = blank

    def fold_plane(plane):
        local[2 + plane].wait()
        fold_pairs(cells, turned, taps, plane)

    def hidden_part(plane, at):
        if plane == 0:
            added = pair_sum(taps, packed, plane, at, 2, range(3))
        else:
            added = early[at] + pair_sum(taps, packed, plane, at, 2, (2,))
        store_hidden(added, held, padded, plane, at, 2)

    def early_sum(at):
        early[at] = pair_sum(taps, packed, 1, at, 2, range(2))

    def fold_rim():
        @pl.when(jnp.logical_not(is_last))
        def _():
            rim.wait_recv()

        @pl.when(is_last)
        def _():
            cells[planes] = jnp.zeros(cells.shape[1:], BF16)
            part_in[...] = jnp.zeros(part_in.shape, BF16)

        fold_pairs(cells, turned, taps, planes)

    def send_rim():
        @pl.when(jnp.logical_not(is_first))
        def _():
            rim.start()

    def sum_for_before(at):
        if at == 0:
            home.wait_recv()
            local[0].wait()
            all_here(2)
        first_unit, columns = lanes[at]
        part_out[:, columns] = third_sum(2, first_unit, blocks, tap, 0, filters).astype(BF16)
        if at == 1:
            @pl.when(jnp.logical_not(is_first))
            def _():
                part.start()

    def sum_of_first(at):
        if at == 0:
            all_here(0)
        first_unit, columns = lanes[at]
        total[:, columns] = third_sum(0, first_unit, blocks, tap, 0, filters)

    def sum_of_second():
        @pl.when(jnp.logical_not(is_last))
        def _():
            part.wait_recv()

        all_here(1)
        for at, columns in lanes:
            added = total[:, columns] + part_in[:, columns].astype(F32)
            out[:, columns] = leaky_relu(third_sum(1, at, blocks, tap, 1, filters) + added).astype(BF16)

    def rims_sent():
        home.wait_send()

        @pl.when(jnp.logical_not(is_first))
        def _():
            rim.wait_send()
            part.wait_send()

    actions = {
        "sent": all_sent, "rims_sent": rims_sent,
        "own": send_own, "home": home.start, "start": start_work, "fold": fold_plane, "hidden": hidden_part, "early": early_sum, "rim": send_rim, "fold_rim": fold_rim,
        "serve": serve, "pass": pass_on, "before": sum_for_before, "first": sum_of_first,
    }
    for name, *at in ORDER:
        actions[name](*at)

    sum_of_second()
    all_sent(1)


def ring_shards(volume, first_filters, second_filters):
    planes, rows, depth, in_channels = volume.shape[1:]
    mid = first_filters.shape[4]
    own = second_filters.shape[4]
    count = lax.axis_size("chan")
    turned_cells = jnp.transpose(volume[0], (0, 1, 3, 2))
    turned_shard = jnp.transpose(second_filters, (0, 1, 2, 4, 3)).reshape(3, 9 * own, mid)
    out_cells = rows // 4 * (depth // 4)
    dma = pltpu.SemaphoreType.DMA
    result = pl.pallas_call(
        ring_kernel,
        out_shape=jax.ShapeDtypeStruct((out_cells, own * count), BF16),
        in_specs=[pl.BlockSpec(memory_space=pl.ANY)] * 3,
        out_specs=whole_vmem(1)[0],
        scratch_shapes=[
            pltpu.VMEM((planes + 1, rows, in_channels, depth), BF16),
            pltpu.VMEM((27, in_channels, mid), BF16),
            pltpu.VMEM((3, 12 * in_channels, mid), BF16),
            pltpu.VMEM((4, depth, 2 * in_channels), F32),
            pltpu.VMEM((planes + 1, rows // 2 + 1, depth // 2, 6 * in_channels), BF16),
            pltpu.VMEM((mid // 128, rows // 4 * (depth // 2), 128), F32),
            pltpu.VMEM((planes // 2, 3, 2, rows // 4 + 1, depth // 4, mid), BF16),
            pltpu.VMEM((3, count, 9 * own, mid), BF16),
            pltpu.VMEM((out_cells, own * count), F32),
            pltpu.VMEM((2, rows // 4 * (depth // 2), mid), F32),
            pltpu.VMEM((out_cells, own * count), BF16),
            pltpu.VMEM((out_cells, own * count), BF16),
            dma((2 + planes,)),
            *[dma((2, 3, count // 4))] * 2,
            *[dma((3, count // 2 - 2))] * 2,
            *[dma((3,))] * 2,
            *[dma((1,))] * 2,
            *[dma((2,))] * 2,
        ],
        compiler_params=pltpu.CompilerParams(
            vmem_limit_bytes=VMEM_BYTES, collective_id=0, has_side_effects=True
        ),
    )(turned_cells, first_filters.reshape(27, in_channels, mid), turned_shard)
    return result.reshape(1, planes // 4, rows // 4, depth // 4, own * count)


def shards(volume, first_filters, second_filters):
    fits = lax.axis_size("chan") == 16 and lax.axis_size("grp") == 2
    if fits and second_filters.shape[4] % 32 == 0 and volume.shape[1] == 4:
        return ring_shards(volume, first_filters, second_filters)
    return plain_shards(volume, first_filters, second_filters)


def solution(mesh):
    placed = (P(("grp", "chan"), None, None, None, None), P(), P(None, None, None, None, "chan"))
    return jax.shard_map(
        shards,
        mesh=mesh,
        in_specs=placed,
        out_specs=P(("grp", "chan"), None, None, None, None),
        check_vma=False,
    )
```

```python
import jax
import jax.numpy as jnp
from jax import lax
from jax.experimental import pallas as pl
from jax.experimental.pallas import tpu as pltpu
from jax.sharding import PartitionSpec as P

F32 = jnp.float32
BF16 = jnp.bfloat16
VMEM_BYTES = 56 * 1024 * 1024


def passed_along(value, axis, steps):
    count = lax.axis_size(axis)
    initial, last = (max(0, -steps), min(count, count - steps))
    return lax.ppermute(value, axis, [(source, source + steps) for source in range(initial, last)])


def leaky_relu(values):
    return jnp.where(values > 0, values, 0.3 * values)


def shifted_up(values, period):
    count = values.shape[0]
    moved = pltpu.roll(values, count - 1, 0)
    row = lax.broadcasted_iota(jnp.int32, values.shape, 0)
    return jnp.where(row % period == period - 1, 0.0, moved)


def taps_of_plane(source, source_plane, taps, plane):
    pairs, depth = source.shape[1] // 2, source.shape[2]

    def body(pair, carry):
        for parity in range(2):
            cells = source[source_plane, 2 * pair + parity]
            moved = shifted_up(cells.astype(F32), depth).astype(BF16)
            taps[plane, parity, pair] = jnp.concatenate([cells, moved], axis=-1)
        return carry

    lax.fori_loop(0, pairs, body, 0)


def zero_row(taps, plane):
    taps[plane, 0, taps.shape[2] - 1] = jnp.zeros(taps.shape[3:], BF16)


def conv_first(taps, filters, held, hidden, plane, part, parts):
    rows = hidden.shape[3] * 2 // parts
    depth, width = taps.shape[3:]
    total = None
    for i in range(3):
        for j in range(3):
            lhs = taps[2 * plane + i, j % 2, pl.ds(part * rows + j // 2, rows)]
            term = jnp.dot(lhs.reshape(rows * depth, width), filters[3 * i + j], preferred_element_type=F32)
            total = term if total is None else total + term
    total = leaky_relu(total).astype(BF16).astype(F32)
    half = rows * depth // 2
    channels = hidden.shape[5]
    blocks = channels // 128
    for block in range(blocks):
        held[block] = total[:, block * 128 : block * 128 + 128]
    for k in range(2):
        cells = jnp.concatenate([held[block, pl.ds(k, half, stride=2)] for block in range(blocks)], axis=-1)
        pieces = [cells] if k else [cells, shifted_up(cells, depth // 2)]
        for at, piece in zip((k, 2), pieces):
            piece = piece.astype(BF16).reshape(rows // 2, 2, depth // 2, channels)
            for parity in range(2):
                hidden[plane, at, parity, pl.ds(part * rows // 2, rows // 2)] = piece[:, parity]


def conv_second(tap, filters, out):
    width = 256 if out.shape[1] % 256 == 0 else out.shape[1]
    for at in range(out.shape[1] // width):
        total = None
        for i in range(3):
            for j in range(3):
                for k in range(3):
                    rhs = filters[9 * i + 3 * j + k, pl.ds(at * width, width)]
                    term = lax.dot_general(
                        tap(i, j, k), rhs, (((1,), (1,)), ((), ())), preferred_element_type=F32
                    )
                    total = term if total is None else total + term
        out[:, pl.ds(at * width, width)] = leaky_relu(total).astype(BF16)


def first_kernel(cells, rim, filters, hidden, taps, held):
    planes = cells.shape[0]
    for plane in range(planes + 1):
        taps_of_plane(cells if plane < planes else rim, plane % planes, taps, plane)
        zero_row(taps, plane)
    for plane in range(planes // 2):
        for part in range(2):
            conv_first(taps, filters, held, hidden, plane, part, 2)


def padded_rows(hidden, rim, padded):
    planes = hidden.shape[0]
    rows = hidden.shape[3]
    for plane in range(planes + 1):
        for k in range(3):
            padded[plane, k, :, pl.ds(0, rows)] = hidden[plane, k] if plane < planes else rim[0, k]
            padded[plane, k, 0, rows] = jnp.zeros(padded.shape[4:], BF16)


def tap_reader(padded, rows):
    depth, channels = padded.shape[4:]

    def tap(i, j, k):
        return padded[i, k, j % 2, pl.ds(j // 2, rows)].reshape(rows * depth, channels)

    return tap


def second_kernel(hidden, rim, filters, out, padded):
    padded_rows(hidden, rim, padded)
    conv_second(tap_reader(padded, hidden.shape[3]), filters, out)


def whole_vmem(count):
    return [pl.BlockSpec(memory_space=pltpu.VMEM)] * count


def padded_first(first_filters):
    kernel, in_channels, out_channels = first_filters.shape[2:]
    flat = first_filters.reshape(9, kernel * in_channels, out_channels)
    return jnp.pad(flat, ((0, 0), (0, in_channels), (0, 0)))


def plain_shards(volume, first_filters, second_filters):
    planes, rows, depth, in_channels = volume.shape[1:]
    mid = first_filters.shape[4]
    turned = jnp.transpose(second_filters, (0, 1, 2, 4, 3)).reshape(27, second_filters.shape[4], mid)
    gathered = lax.all_gather(turned, "chan", axis=1, tiled=True)
    cells = volume.reshape(planes, rows, depth // 2, 2 * in_channels)
    rim = passed_along(cells[:1], "chan", -1)
    filters = padded_first(first_filters)
    hidden_shape = (planes // 2, 3, 2, rows // 4, depth // 4, mid)
    hidden = pl.pallas_call(
        first_kernel,
        out_shape=jax.ShapeDtypeStruct(hidden_shape, BF16),
        in_specs=whole_vmem(3),
        out_specs=whole_vmem(1)[0],
        scratch_shapes=[
            pltpu.VMEM((planes + 1, 2, rows // 2 + 1, depth // 2, 4 * in_channels), BF16),
            pltpu.VMEM((mid // 128, rows // 4 * (depth // 2), 128), F32),
        ],
        compiler_params=pltpu.CompilerParams(vmem_limit_bytes=VMEM_BYTES),
    )(cells, rim, filters)
    hidden_rim = passed_along(hidden[:1], "chan", -1)
    out_cells = rows // 4 * (depth // 4)
    out_channels = gathered.shape[1]
    result = pl.pallas_call(
        second_kernel,
        out_shape=jax.ShapeDtypeStruct((out_cells, out_channels), BF16),
        in_specs=whole_vmem(3),
        out_specs=whole_vmem(1)[0],
        scratch_shapes=[
            pltpu.VMEM((planes // 2 + 1, 3, 2, rows // 4 + 1, depth // 4, mid), BF16),
        ],
        compiler_params=pltpu.CompilerParams(vmem_limit_bytes=VMEM_BYTES),
    )(hidden, hidden_rim, gathered)
    return result.reshape(1, planes // 4, rows // 4, depth // 4, out_channels)


def position_of(chip, chips):
    column, along = chip % 2, chip // 2
    return along * (1 - column) + (chips - 1 - along) * column


def chip_at(position, chips):
    upper = position // (chips // 2)
    return (1 - upper) * 2 * position + upper * (2 * (chips - 1 - position) + 1)


def fold_pairs(cells, turned, taps, plane):
    pairs = cells.shape[1] // 2
    channels, depth = cells.shape[2:]
    slots = turned.shape[0]

    def body(step, carry):
        for slot in range(slots):
            pair = step * slots + slot
            both = cells[plane, pl.ds(2 * pair, 2)].reshape(2 * channels, depth)
            turned[slot] = both.astype(F32).T
            even = turned[slot, pl.ds(0, depth // 2, stride=2)]
            odd = turned[slot, pl.ds(1, depth // 2, stride=2)]
            later = shifted_up(even, depth // 2)
            taps[plane, pair] = jnp.concatenate([even, odd, later], axis=-1).astype(BF16)
        return carry

    lax.fori_loop(0, pairs // slots, body, 0)
    taps[plane, pairs] = jnp.zeros(taps.shape[2:], BF16)


def pack_first(filters, packed):
    channels, out_channels = filters.shape[1:]
    for i in range(3):
        for k in range(3):
            for j in range(2):
                packed[i, pl.ds((2 * k + j) * channels, channels)] = filters[9 * i + 3 * j + k]
            packed[i, pl.ds((6 + 2 * k) * channels, channels)] = filters[9 * i + 6 + k]
            packed[i, pl.ds((7 + 2 * k) * channels, channels)] = jnp.zeros((channels, out_channels), BF16)


def pair_sum(taps, packed, plane, part, parts, offsets):
    rows = (taps.shape[1] - 1) // parts
    depth, width = taps.shape[2:]
    total = None
    for i in offsets:
        here = taps[2 * plane + i, pl.ds(part * rows, rows)].reshape(rows * depth, width)
        below = taps[2 * plane + i, pl.ds(part * rows + 1, rows)].reshape(rows * depth, width)
        lhs = jnp.concatenate([here, below], axis=-1)
        term = jnp.dot(lhs, packed[i], preferred_element_type=F32)
        total = term if total is None else total + term
    return total


def store_hidden(total, held, padded, plane, part, parts):
    depth = 2 * padded.shape[4]
    rows = total.shape[0] // depth
    channels = total.shape[1]
    total = leaky_relu(total).astype(BF16).astype(F32)
    half = rows * depth // 2
    blocks = channels // 128
    for block in range(blocks):
        held[block] = total[:, block * 128 : block * 128 + 128]
    for k in range(2):
        cells = jnp.concatenate([held[block, pl.ds(k, half, stride=2)] for block in range(blocks)], axis=-1)
        pieces = [cells] if k else [cells, shifted_up(cells, depth // 2)]
        for at, piece in zip((k, 2), pieces):
            piece = piece.astype(BF16).reshape(rows // 2, 2, depth // 2, channels)
            for parity in range(2):
                padded[plane, at, parity, pl.ds(part * rows // 2, rows // 2)] = piece[:, parity]


ORDER = (
    ("own", 2), ("home",), ("start",), ("own", 0), ("fold", 1), ("own", 1), ("fold", 2), ("serve", 2, 1),
    ("serve", 0, 1), ("serve", 1, 1), ("hidden", 0, 0), ("serve", 2, 2), ("pass", 2, 1), ("rim",), ("serve", 0,
    2), ("pass", 0, 1), ("hidden", 0, 1), ("serve", 2, 3), ("pass", 1, 1), ("fold", 3), ("early", 0), ("serve",
    1, 2), ("pass", 2, 2), ("early", 1), ("serve", 2, 4), ("pass", 0, 2), ("serve", 0, 3), ("pass", 2, 3),
    ("serve", 1, 3), ("pass", 1, 2), ("before", 0), ("before", 1), ("serve", 0, 4), ("fold_rim",), ("serve", 1,
    4), ("pass", 0, 3), ("hidden", 1, 0), ("hidden", 1, 1), ("pass", 1, 3), ("first", 0), ("first", 1),
)


def third_sum(i, lanes, blocks, tap, plane, filters):
    own_rows = filters.shape[2] // 9
    added = None
    for j in range(3):
        for k in range(3):
            rhs = filters[i, pl.ds(lanes, blocks), pl.ds((3 * j + k) * own_rows, own_rows)]
            term = lax.dot_general(
                tap(plane, j, k), rhs.reshape(blocks * own_rows, rhs.shape[2]), (((1,), (1,)), ((), ())),
                preferred_element_type=F32,
            )
            added = term if added is None else added + term
    return added


def ring_kernel(
    volume, first, shard, out,
    cells, first_held, packed, turned, taps, held, padded, filters, total, early, part_out, part_in,
    local_sem, ring_send, ring_recv, cross_send, cross_recv, side_send, side_recv,
    home_send, home_recv, rim_send, rim_recv,
):
    count = lax.axis_size("chan")
    chips = count // 2
    me = lax.axis_index("chan")
    grp = lax.axis_index("grp")
    core, chip = me % 2, me // 2
    spot = position_of(chip, chips)
    sibling = me + 1 - 2 * core
    right = 2 * chip_at((spot + 1) % chips, chips) + core
    left = 2 * chip_at((spot + chips - 1) % chips, chips) + core
    before, after = (me + count - 1) % count, (me + 1) % count
    planes = volume.shape[0]
    far = chips // 2
    piece = shard.shape[1]
    carried = piece * 10 // 18
    crossed = piece - carried
    halves = (160, piece - 160)
    is_first, is_last = me == 0, me == count - 1

    local = [pltpu.make_async_copy(shard, filters.at[:, me], local_sem.at[0])]
    local.append(pltpu.make_async_copy(first, first_held, local_sem.at[1]))
    for plane in range(planes):
        local.append(pltpu.make_async_copy(volume.at[plane], cells.at[plane], local_sem.at[2 + plane]))
    for copy in local[1:3]:
        copy.start()

    barrier = pltpu.get_barrier_semaphore()
    peers = [{"chan": peer} for peer in (left, right, sibling, before, after)] + [{"grp": 1 - grp}]
    for peer in peers:
        pl.semaphore_signal(barrier, inc=1, device_id=peer, device_id_type=pl.DeviceIdType.MESH)
    pl.semaphore_wait(barrier, len(peers))

    def remote(source, target, send, recv, peer):
        return pltpu.make_async_remote_copy(
            src_ref=source, dst_ref=target, send_sem=send, recv_sem=recv,
            device_id=peer, device_id_type=pl.DeviceIdType.MESH,
        )

    def rows_at(offset, size):
        return pl.ds(pl.multiple_of(offset, 16), size)

    def unit_of(way, gone):
        return 2 * chip_at((spot + (chips - gone if way == 0 else gone)) % chips, chips) + core

    def ring_rows(way, gone):
        upper = grp if way == 0 else 1 - grp
        if gone < far:
            return rows_at(upper * crossed, carried)
        return rows_at(upper * (piece - halves[way]), halves[way])

    def ring(way, t, gone):
        unit, rows = unit_of(way, gone - 1), ring_rows(way, gone)
        target = filters.at[t, unit, rows]
        source = shard.at[t, rows] if gone == 1 else target
        return remote(
            source, target, ring_send.at[way, t, gone - 1], ring_recv.at[way, t, gone - 1],
            {"chan": (right, left)[way]},
        )

    def arrival(way, t, gone):
        target = filters.at[t, unit_of(way, gone), ring_rows(way, gone)]
        return remote(
            target, target, ring_send.at[way, t, gone - 1], ring_recv.at[way, t, gone - 1], {"chan": left}
        )

    def cross(way, t, gone):
        upper = grp if way == 0 else 1 - grp
        block = filters.at[t, unit_of(way, gone), rows_at(upper * carried, crossed)]
        at = 2 * (gone - 1) + way
        return remote(block, block, cross_send.at[t, at], cross_recv.at[t, at], {"grp": 1 - grp})

    def side(way, t, gone):
        block = filters.at[t, unit_of(way, gone)]
        return remote(block, block, side_send.at[t], side_recv.at[t], {"chan": sibling})

    home = remote(shard, filters.at[:, me], home_send.at[0], home_recv.at[0], {"chan": sibling})
    rim = remote(volume.at[0], cells.at[planes], rim_send.at[0], rim_recv.at[0], {"chan": before})
    part = remote(part_out, part_in, rim_send.at[1], rim_recv.at[1], {"chan": before})

    for copy in local[3:] + local[:1]:
        copy.start()

    def send_own(t):
        for way in range(2):
            ring(way, t, 1).start()

    def serve(t, gone):
        for way in (1, 0):
            arrival(way, t, gone).wait_recv()
            if gone < far:
                cross(way, t, gone).start()
                ring(way, t, gone + 1).start()
        if gone == far:
            side(0, t, gone).start()

    def pass_on(t, gone):
        for way in range(2 if gone < far else 0):
            cross(way, t, gone).wait_recv()
            side(way, t, gone).start()

    def all_sides(t):
        block = filters.at[t, pl.ds(0, chips - 1)]
        return remote(block, block, side_send.at[t], side_recv.at[t], {"chan": sibling})

    def all_here(t):
        all_sides(t).wait_recv()

    def all_sent(t):
        for way in range(2):
            for gone in range(1, far + 1):
                ring(way, t, gone).wait_send()
            for gone in range(1, far):
                cross(way, t, gone).wait_send()
        all_sides(t).wait_send()

    tap = tap_reader(padded, padded.shape[3] - 1)
    blocks = filters.shape[1] // 2
    half = blocks * shard.shape[1] // 9
    lanes = [(at * blocks, pl.ds(at * half, half)) for at in range(2)]

    def start_work():
        local[1].wait()
        pack_first(first_held, packed)
        local[2].wait()
        fold_pairs(cells, turned, taps, 0)
        blank = jnp.zeros(padded.shape[4:], BF16)
        for plane in range(planes // 2):
            for k in range(3):
                padded[plane, k, 0, padded.shape[3] - 1] = blank

    def fold_plane(plane):
        local[2 + plane].wait()
        fold_pairs(cells, turned, taps, plane)

    def hidden_part(plane, at):
        if plane == 0:
            added = pair_sum(taps, packed, plane, at, 2, range(3))
        else:
            added = early[at] + pair_sum(taps, packed, plane, at, 2, (2,))
        store_hidden(added, held, padded, plane, at, 2)

    def early_sum(at):
        early[at] = pair_sum(taps, packed, 1, at, 2, range(2))

    def fold_rim():
        @pl.when(jnp.logical_not(is_last))
        def _():
            rim.wait_recv()

        @pl.when(is_last)
        def _():
            cells[planes] = jnp.zeros(cells.shape[1:], BF16)
            part_in[...] = jnp.zeros(part_in.shape, BF16)

        fold_pairs(cells, turned, taps, planes)

    def send_rim():
        @pl.when(jnp.logical_not(is_first))
        def _():
            rim.start()

    def sum_for_before(at):
        if at == 0:
            home.wait_recv()
            local[0].wait()
            all_here(2)
        first_unit, columns = lanes[at]
        part_out[:, columns] = third_sum(2, first_unit, blocks, tap, 0, filters).astype(BF16)
        if at == 1:
            @pl.when(jnp.logical_not(is_first))
            def _():
                part.start()

    def sum_of_first(at):
        if at == 0:
            all_here(0)
        first_unit, columns = lanes[at]
        total[:, columns] = third_sum(0, first_unit, blocks, tap, 0, filters)

    def sum_of_second():
        @pl.when(jnp.logical_not(is_last))
        def _():
            part.wait_recv()

        all_here(1)
        for at, columns in lanes:
            added = total[:, columns] + part_in[:, columns].astype(F32)
            out[:, columns] = leaky_relu(third_sum(1, at, blocks, tap, 1, filters) + added).astype(BF16)

    actions = {
        "own": send_own, "home": home.start, "start": start_work, "fold": fold_plane, "hidden": hidden_part, "early": early_sum, "rim": send_rim, "fold_rim": fold_rim,
        "serve": serve, "pass": pass_on, "before": sum_for_before, "first": sum_of_first,
    }
    for name, *at in ORDER:
        actions[name](*at)

    sum_of_second()
    for t in range(3):
        all_sent(t)
    home.wait_send()

    @pl.when(jnp.logical_not(is_first))
    def _():
        rim.wait_send()
        part.wait_send()


def ring_shards(volume, first_filters, second_filters):
    planes, rows, depth, in_channels = volume.shape[1:]
    mid = first_filters.shape[4]
    own = second_filters.shape[4]
    count = lax.axis_size("chan")
    turned_cells = jnp.transpose(volume[0], (0, 1, 3, 2))
    turned_shard = jnp.transpose(second_filters, (0, 1, 2, 4, 3)).reshape(3, 9 * own, mid)
    out_cells = rows // 4 * (depth // 4)
    dma = pltpu.SemaphoreType.DMA
    result = pl.pallas_call(
        ring_kernel,
        out_shape=jax.ShapeDtypeStruct((out_cells, own * count), BF16),
        in_specs=[pl.BlockSpec(memory_space=pl.ANY)] * 3,
        out_specs=whole_vmem(1)[0],
        scratch_shapes=[
            pltpu.VMEM((planes + 1, rows, in_channels, depth), BF16),
            pltpu.VMEM((27, in_channels, mid), BF16),
            pltpu.VMEM((3, 12 * in_channels, mid), BF16),
            pltpu.VMEM((4, depth, 2 * in_channels), F32),
            pltpu.VMEM((planes + 1, rows // 2 + 1, depth // 2, 6 * in_channels), BF16),
            pltpu.VMEM((mid // 128, rows // 4 * (depth // 2), 128), F32),
            pltpu.VMEM((planes // 2, 3, 2, rows // 4 + 1, depth // 4, mid), BF16),
            pltpu.VMEM((3, count, 9 * own, mid), BF16),
            pltpu.VMEM((out_cells, own * count), F32),
            pltpu.VMEM((2, rows // 4 * (depth // 2), mid), F32),
            pltpu.VMEM((out_cells, own * count), BF16),
            pltpu.VMEM((out_cells, own * count), BF16),
            dma((2 + planes,)),
            *[dma((2, 3, count // 4))] * 2,
            *[dma((3, count // 2 - 2))] * 2,
            *[dma((3,))] * 2,
            *[dma((1,))] * 2,
            *[dma((2,))] * 2,
        ],
        compiler_params=pltpu.CompilerParams(
            vmem_limit_bytes=VMEM_BYTES, collective_id=0, has_side_effects=True
        ),
    )(turned_cells, first_filters.reshape(27, in_channels, mid), turned_shard)
    return result.reshape(1, planes // 4, rows // 4, depth // 4, own * count)


def shards(volume, first_filters, second_filters):
    fits = lax.axis_size("chan") == 16 and lax.axis_size("grp") == 2
    if fits and second_filters.shape[4] % 32 == 0 and volume.shape[1] == 4:
        return ring_shards(volume, first_filters, second_filters)
    return plain_shards(volume, first_filters, second_filters)


def solution(mesh):
    placed = (P(("grp", "chan"), None, None, None, None), P(), P(None, None, None, None, "chan"))
    return jax.shard_map(
        shards,
        mesh=mesh,
        in_specs=placed,
        out_specs=P(("grp", "chan"), None, None, None, None),
        check_vma=False,
    )
```
